32 devices in a mesh: groups: 2 (over x), prompt: 8 (over z, y), resp: 2 (over core).
Axes of the slice: x: 2, y: 2, z: 4, core: 2. Of those that a mesh axis runs over, the one named last changes fastest.
Arguments:
- queries: bfloat16 [16, 512, 1024], P(('groups', 'prompt'), 'resp'), parts along dimension 0, may hold values from -4096 to 4096
- grad_out: bfloat16 [16, 512, 1024], P(('groups', 'prompt'), 'resp'), parts along dimension 0, may hold values from -48 to 48
- keys_resp: bfloat16 [16, 512, 128], P(('groups', 'prompt'), 'resp'), parts along dimension 0, may hold values from -6 to 6
- values_resp: bfloat16 [16, 512, 128], P(('groups', 'prompt'), 'resp'), parts along dimension 0, may hold values from -6 to 6
- keys_prefix: bfloat16 [1024, 128], P(('groups', 'prompt')), parts along dimension 0, may hold values from -32 to 32
- values_prefix: bfloat16 [1024, 128], P(('groups', 'prompt')), parts along dimension 0, may hold values from -6 to 6
- lengths: int32 [16], P(('groups', 'prompt')), parts along dimension 0, may hold values from 1 to 512, as said below
- block_plan: int32 [16, 4], P(('groups', 'prompt'), 'resp'), parts along dimension 0, may hold values from 0 to 3, as said below
Outputs:
- query_grads: float32 [16, 512, 1024], P(('groups', 'prompt'), 'resp'), parts along dimension 0
- prefix_keygrad: float32 [1024, 128], P(('groups', 'prompt', 'resp')), parts along dimension 0
- prefix_valgrad: float32 [1024, 128], P(('groups', 'prompt', 'resp')), parts along dimension 0
- reply_keygrad: float32 [16, 512, 128], P(('groups', 'prompt'), 'resp'), parts along dimension 0
- reply_valgrad: float32 [16, 512, 128], P(('groups', 'prompt'), 'resp'), parts along dimension 0
The draws below stay inside these ranges and needn't reach their ends.
There are 2 independent parts, one for each index of `groups`. The reference program is written for one: setup_inputs(seed, part) draws one part's arguments, and reference() takes and returns one part's arrays. A program takes and returns all parts, laid end to end along the dimension named above; each array names one. Nothing has to cross between parts.
Inputs may be any that keep to these rules, and one draw needn't show every extreme that they name: `lengths`: one response has exactly 512 live positions. `block_plan`: each row is a permutation of 0 to 3; for every m, blocks 2 * m and 2 * m + 1 stand in different halves of the row.
All inputs are finite; a program needn't handle non-finite values.
Results may differ from the reference program's by a relative error of at most 0.0029.
Values may be sent and summed in bfloat16 or wider, within the bound.
A program may use at most 64 MiB of HBM per device.

```python
import jax
import jax.numpy as jnp
from jax import lax

HEAD = 128
HEADS = 8
RBLK = 128
P_SIZE = 512
NRESP = 8
LMAX = 512
NBLK = 4


def prefix_draw(key):
    normal_draw = jnp.clip(jax.random.normal(jax.random.fold_in(key, 101), (P_SIZE, HEAD), jnp.float32), -5.0, 5.0)
    return normal_draw


def draw_keys_prefix(key, part):
    return prefix_draw(key).astype(jnp.bfloat16)


def draw_queries(key, part):
    normal_draw = jnp.clip(jax.random.normal(jax.random.fold_in(key, 201), (NRESP, LMAX, HEADS, HEAD), jnp.float32), -5.0, 5.0)
    return normal_draw.reshape(NRESP, LMAX, HEADS * HEAD).astype(jnp.bfloat16)


def draw_lengths(key, part):
    lengths_draw = jax.random.randint(jax.random.fold_in(key, 401), (NRESP,), 1, LMAX + 1, jnp.int32)
    longest = jax.random.randint(jax.random.fold_in(key, 402), (), 0, NRESP, jnp.int32)
    return jnp.where(jnp.arange(NRESP, dtype=jnp.int32) == longest, LMAX, lengths_draw).astype(jnp.int32)


def draw_block_plan(key, part):
    half_count = NBLK // 2
    coin_flip = jax.random.randint(jax.random.fold_in(key, 301), (NRESP, half_count), 0, 2, jnp.int32)
    pair_start = 2 * jnp.arange(half_count, dtype=jnp.int32)
    to_first = pair_start[None, :] + coin_flip
    to_second = pair_start[None, :] + 1 - coin_flip
    halves = jnp.stack([to_first, to_second], 1)
    subkeys = jax.random.split(jax.random.fold_in(key, 302), NRESP * 2)
    orders = jax.vmap(lambda subkey: jax.random.permutation(subkey, half_count))(subkeys).reshape(NRESP, 2, half_count)
    placed = jnp.take_along_axis(halves, orders.astype(jnp.int32), axis=2)
    return placed.reshape(NRESP, NBLK).astype(jnp.int32)


def shard_levels(key, dims, cuts, least, top_value):
    loudness = 1.0
    for dim, parts in cuts:
        draws = jax.random.uniform(jax.random.fold_in(jax.random.fold_in(key, 6), dim), (parts,), jnp.float32, least / len(cuts), top_value / len(cuts))
        loudness = loudness * jnp.repeat(jnp.exp(draws), dims[dim] // parts).reshape((-1,) + (1,) * (len(dims) - 1 - dim))
    return loudness


def noise(rng, extent, deviation, most, cuts=(), held_as=jnp.bfloat16):
    values = jax.random.normal(rng, extent, jnp.float32) * deviation
    if len(cuts) > 0:
        values = shard_levels(rng, extent, cuts, -0.22, 0.18) * values
    return jnp.clip(values, min=-most, max=most).astype(held_as)


def setup_inputs(seed: int = 0, part: int = 0) -> dict:
    arg_keys = jax.random.split(jax.random.key(seed), 9)
    part_keys = jax.random.split(jax.random.fold_in(arg_keys[8], part), 9)
    return {
        "queries": draw_queries(jax.random.fold_in(jax.random.fold_in(arg_keys[8], part), 71), part),
        "grad_out": noise(part_keys[1], (NRESP, LMAX, HEADS * HEAD), 8.0, 48.0, ((0, 8), (1, 2))),
        "keys_resp": noise(part_keys[2], (NRESP, LMAX, HEAD), 1.0, 6.0, ((0, 8), (1, 2))),
        "values_resp": noise(part_keys[3], (NRESP, LMAX, HEAD), 1.0, 6.0, ((0, 8), (1, 2))),
        "keys_prefix": draw_keys_prefix(jax.random.fold_in(jax.random.fold_in(arg_keys[8], part), 71), part),
        "values_prefix": noise(part_keys[5], (P_SIZE, HEAD), 1.0, 6.0, ((0, 8),)),
        "lengths": draw_lengths(jax.random.fold_in(jax.random.fold_in(arg_keys[8], part), 71), part),
        "block_plan": draw_block_plan(jax.random.fold_in(jax.random.fold_in(arg_keys[8], part), 71), part),
    }


def reference(queries, grad_out, keys_resp, values_resp, keys_prefix, values_prefix, lengths, block_plan):
    score_scale = HEAD ** -0.5
    prefix_keys = keys_prefix.astype(jnp.float32)
    prefix_values = values_prefix.astype(jnp.float32)
    key_index = jnp.arange(P_SIZE + LMAX, dtype=jnp.int32)
    relative = key_index - P_SIZE
    positions = jnp.arange(LMAX, dtype=jnp.int32)

    def per_response(totals, block_item):
        query_rows, grad_rows, reply_keys, reply_values, length = block_item
        all_keys = jnp.concatenate([prefix_keys, reply_keys.astype(jnp.float32)], 0)
        all_values = jnp.concatenate([prefix_values, reply_values.astype(jnp.float32)], 0)
        query_heads = query_rows.astype(jnp.float32).reshape(LMAX, HEADS, HEAD)
        live_rows = positions < length
        grad_heads = jnp.where(live_rows[:, None, None], grad_rows.astype(jnp.float32).reshape(LMAX, HEADS, HEAD), jnp.float32(0.0))
        visible = (key_index[None, :] < P_SIZE) | ((relative[None, :] <= positions[:, None]) & (relative[None, :] < length))
        scores = jnp.einsum('rhd,kd->rhk', query_heads, all_keys) * score_scale
        scores = jnp.where(visible[:, None, :], scores, -jnp.inf)
        row_max = jnp.max(scores, -1, keepdims=True)
        exponent = jnp.exp(scores - row_max)
        weights = exponent / jnp.sum(exponent, -1, keepdims=True)
        grad_weight = jnp.einsum('rhd,kd->rhk', grad_heads, all_values)
        row_inner = jnp.sum(weights * grad_weight, -1, keepdims=True)
        grad_score = lax.optimization_barrier((weights * (grad_weight - row_inner)).astype(jnp.bfloat16)).astype(jnp.float32)
        rounded_weights = lax.optimization_barrier(weights.astype(jnp.bfloat16)).astype(jnp.float32)
        grad_q = jnp.einsum('rhk,kd->rhd', grad_score, all_keys) * score_scale
        grad_k = jnp.einsum('rhk,rhd->kd', grad_score, query_heads) * score_scale
        grad_v = jnp.einsum('rhk,rhd->kd', rounded_weights, grad_heads)
        new_totals = (totals[0] + grad_k[:P_SIZE], totals[1] + grad_v[:P_SIZE])
        return new_totals, (grad_q.reshape(LMAX, HEADS * HEAD), grad_k[P_SIZE:], grad_v[P_SIZE:])

    zeros = jnp.zeros((P_SIZE, HEAD), jnp.float32)
    totals, outputs = lax.scan(per_response, (zeros, zeros), (queries, grad_out, keys_resp, values_resp, lengths))
    natural_grads, reply_keygrad, reply_valgrad = outputs
    blocks = natural_grads.reshape(NRESP, NBLK, RBLK, HEADS * HEAD)
    chosen = jnp.take_along_axis(blocks, block_plan.astype(jnp.int32)[:, :, None, None], axis=1)
    query_grads = chosen.reshape(NRESP, LMAX, HEADS * HEAD)
    return query_grads, totals[0], totals[1], reply_keygrad, reply_valgrad
```

```python
import functools
import math

import jax
import jax.numpy as jnp
from jax import lax
from jax.experimental import pallas as pl
from jax.experimental.pallas import tpu as pltpu
from jax.sharding import PartitionSpec as P

RBLK = 128
CHUNK = 256
HIDDEN = -1e30
MESH = pl.DeviceIdType.MESH
F32 = jnp.float32
BF16 = jnp.bfloat16


def remote(src, dst, send_sem, recv_sem, device):
    return pltpu.make_async_remote_copy(
        src_ref=src,
        dst_ref=dst,
        send_sem=send_sem,
        recv_sem=recv_sem,
        device_id=device,
        device_id_type=MESH,
    )


def dot_nt(a, b):
    return lax.dot_general(a, b, (((1,), (1,)), ((), ())), preferred_element_type=F32)


def dot_nn(a, b):
    return lax.dot_general(a, b, (((1,), (0,)), ((), ())), preferred_element_type=F32)


def kernel(
    chips, heads, lean,
    len_hbm, plan_hbm, q_hbm, g_hbm, kr_hbm, vr_hbm, kp_hbm, vp_hbm,
    dq, pk_out, pv_out, rk_out, rv_out,
    len_ref, plan_ref, raw, sb, wk, kv, kt, ep, gp, pt, dt, pr, dr, er, gr, stat, fac, inn,
    tb, rb, s2, r2, rt, rr,
    local_sem, pair_send, pair_recv, gat_send, gat_recv, fwd_send, fwd_recv,
    sum_send, sum_recv, out_send, out_recv,
):
    me = lax.axis_index("prompt")
    core = lax.axis_index("resp")
    partner = {"resp": 1 - core}
    shard = kp_hbm.shape[0]
    half = shard // 2
    prefix_len = chips * shard
    own_keys = kr_hbm.shape[1]
    width = raw.shape[3]
    steps = width // CHUNK
    scale = kv.shape[2] ** (-0.5)
    soft = scale * math.log2(math.e)
    square = chips & (chips - 1) == 0

    def target(k):
        return lax.bitwise_xor(me, k) if square else lax.rem(me + k, chips)

    def source(k):
        return lax.bitwise_xor(me, k) if square else lax.rem(me + chips - k, chips)

    barrier = pltpu.get_barrier_semaphore()
    for k in range(chips - 1, 0, -1):
        pl.semaphore_signal(barrier, inc=1, device_id={"prompt": target(k)}, device_id_type=MESH)
    pl.semaphore_signal(barrier, inc=1, device_id=partner, device_id_type=MESH)

    own_rows = pl.ds(pl.multiple_of(prefix_len + core * own_keys, own_keys), own_keys)
    loads = [
        pltpu.make_async_copy(len_hbm, len_ref, local_sem.at[0]),
        pltpu.make_async_copy(plan_hbm, plan_ref, local_sem.at[1]),
        pltpu.make_async_copy(q_hbm, raw.at[0], local_sem.at[2]),
        pltpu.make_async_copy(g_hbm, raw.at[1], local_sem.at[3]),
        pltpu.make_async_copy(kr_hbm.at[0], kv.at[0, own_rows], local_sem.at[4]),
        pltpu.make_async_copy(vr_hbm.at[0], kv.at[1, own_rows], local_sem.at[5]),
        pltpu.make_async_copy(kp_hbm, kv.at[0, :shard], local_sem.at[6]),
        pltpu.make_async_copy(vp_hbm, kv.at[1, :shard], local_sem.at[7]),
    ]
    for load in loads:
        load.start()
    for load in loads:
        load.wait()

    length = len_ref[0]
    first, second = plan_ref[0, 0], plan_ref[0, 1]
    own_block = jnp.where(first // 2 == core, first, second)
    other_block = jnp.where(first // 2 == core, second, first)
    own_local = lax.rem(own_block, 2)
    sent_local = 1 - own_local
    sent_block = 2 * core + sent_local
    blocks_of = (
        jnp.where(core == 0, own_block, other_block),
        jnp.where(core == 0, other_block, own_block),
    )
    place_of = (core, 1 - core)

    def stack(block_local, block, put):
        rows = lax.broadcasted_iota(jnp.int32, (RBLK, 128), 0) + block * RBLK
        live = rows < length
        for h in range(heads):
            lanes = slice(h * 128, (h + 1) * 128)
            put[0, :, lanes] = raw[0, block_local, :, lanes].T
            grads = raw[1, block_local, :, lanes]
            put[1, :, lanes] = jnp.where(live, grads, jnp.zeros_like(grads)).T

    def lanes_of(j):
        return pl.ds(pl.multiple_of(j * CHUNK, CHUNK), CHUNK)

    def note(level, row, lanes, top, e, gw):
        stat[0, level, row : row + 1, lanes] = top
        stat[1, level, row : row + 1, lanes] = jnp.sum(e, 0, keepdims=True)
        stat[2, level, row : row + 1, lanes] = jnp.sum(e * gw, 0, keepdims=True)

    def piece(place, level, block, part, slot, row):
        keys = pl.ds(pl.multiple_of(prefix_len + part * own_keys, own_keys), own_keys)

        def step(j, carry):
            lanes = lanes_of(j)
            lane = lax.broadcasted_iota(jnp.int32, (1, CHUNK), 1)
            limit = jnp.minimum(block * RBLK + lax.rem(lane, RBLK), length - 1)
            spot = lax.broadcasted_iota(jnp.int32, (own_keys, CHUNK), 0) + part * own_keys
            scores = dot_nn(kv[0, keys], wk[place, 0, :, lanes])
            scores = jnp.where(spot <= limit, scores, HIDDEN)
            top = jnp.max(scores, 0, keepdims=True)
            e = jnp.exp2((scores - top) * soft)
            gw = dot_nn(kv[1, keys], wk[place, 1, :, lanes])
            er[slot, :, lanes] = e
            gr[slot, :, lanes] = gw
            note(level, row, lanes, top, e, gw)
            return carry

        lax.fori_loop(0, steps, step, 0, unroll=True)

    def shard_pass(k, place, level):
        keys = slice(k * shard, (k + 1) * shard)

        def step(j, carry):
            lanes = lanes_of(j)
            scores = dot_nn(kv[0, keys], wk[place, 0, :, lanes])
            top = jnp.max(scores, 0, keepdims=True)
            e = jnp.exp2((scores - top) * soft)
            gw = dot_nn(kv[1, keys], wk[place, 1, :, lanes])
            ep[level, keys, lanes] = e
            if not lean:
                gp[level, keys, lanes] = gw
            note(level, k, lanes, top, e, gw)
            return carry

        lax.fori_loop(0, steps, step, 0, unroll=True)

    stack(sent_local, sent_block, sb)
    stack(own_local, own_block, wk.at[0])
    piece(0, core, own_block, core, 2 * core, chips)
    shard_pass(0, 0, core)

    pl.semaphore_wait(barrier, chips)

    def slot_rows(k):
        return kv.at[:, k * shard : (k + 1) * shard]

    @pl.when(core == 1)
    def _():
        for k in range(chips - 1, 0, -1):
            remote(
                slot_rows(0), slot_rows(k), gat_send.at[k], gat_recv.at[k], {"prompt": target(k)}
            ).start()

    pair_kv = remote(
        kv.at[:, own_rows], kv.at[:, own_rows], pair_send.at[0], pair_recv.at[0], partner
    )
    pair_kv.start()
    pair_q = remote(sb, wk.at[1], pair_send.at[1], pair_recv.at[1], partner)
    pair_q.start()
    pair_kv.wait_recv()
    pair_q.wait_recv()
    piece(1 - core, 1, blocks_of[1], 0, 1, chips + 1)
    piece(1, 1 - core, other_block, 1 - core, 2 * (1 - core), chips)
    shard_pass(0, 1, 1 - core)

    def forward(k):
        return remote(slot_rows(k), slot_rows(k), fwd_send.at[k], fwd_recv.at[k], partner)

    for k in range(chips - 1, 0, -1):

        @pl.when(core == 1)
        def _():
            remote(
                slot_rows(k), slot_rows(k), gat_send.at[k], gat_recv.at[k], {"prompt": source(k)}
            ).wait_recv()
            forward(k).start()

        @pl.when(core == 0)
        def _():
            forward(k).wait_recv()

        for level in range(2):
            shard_pass(k, place_of[level], level)

    for level in range(2):
        rows = slice(0, chips + 1 + level)

        def combine(j, carry):
            lanes = lanes_of(j)
            tops = stat[0, level, rows, lanes]
            factors = jnp.exp2((tops - jnp.max(tops, 0, keepdims=True)) * soft)
            inv = 1.0 / jnp.sum(factors * stat[1, level, rows, lanes], 0, keepdims=True)
            inner = jnp.sum(factors * stat[2, level, rows, lanes], 0, keepdims=True) * inv
            fac[level, rows, lanes] = factors * inv
            inn[level, :, lanes] = inner
            return carry

        lax.fori_loop(0, steps, combine, 0, unroll=True)

    def scaled(n):
        for level in range(2):
            for k in range(n * per, (n + 1) * per):
                keys = slice(k * shard, (k + 1) * shard)

                def step(j, carry):
                    lanes = lanes_of(j)
                    if lean:
                        gw = dot_nn(kv[1, keys], wk[place_of[level], 1, :, lanes])
                    else:
                        gw = gp[level, keys, lanes]
                    weights = ep[level, keys, lanes] * fac[level, k : k + 1, lanes]
                    pt[level, keys, lanes] = weights.astype(BF16)
                    dt[level, keys, lanes] = (weights * (gw - inn[level, :, lanes])).astype(BF16)
                    return carry

                lax.fori_loop(0, steps, step, 0, unroll=True)

    def totals(weights, grads, items):
        k_sum = v_sum = None
        for i, rows, level in items:
            place = place_of[level]
            k_part = dot_nt(wk[place, 0], grads[i, rows, :])
            v_part = dot_nt(wk[place, 1], weights[i, rows, :])
            k_sum = k_part if k_sum is None else k_sum + k_part
            v_sum = v_part if v_sum is None else v_sum + v_part
        return (k_sum * scale).T, v_sum.T

    per = 256 // shard
    count = chips // per
    sums = {}
    for n in range(count - 1, -1, -1):
        scaled(n)
        rows = slice(n * 256, (n + 1) * 256)
        k_sum, v_sum = totals(pt, dt, [(level, rows, level) for level in range(2)])
        span = pl.ds(n * per, per)
        for which, value in ((0, k_sum), (1, v_sum)):
            value = value.reshape(per, 2, half, 128)
            for c in range(2):
                tb[c, span, which] = value[:, c]
        sums[n] = remote(
            tb.at[1 - core, span], rb.at[span], sum_send.at[n], sum_recv.at[n], partner
        )
        sums[n].start()

    def send_out(n):
        sums[n].wait_recv()
        span = pl.ds(n * per, per)
        s2[span] = (tb[core, span] + rb[span]).astype(BF16)
        for k in range((n + 1) * per - 1, n * per - 1, -1):
            if k > 0:
                remote(
                    s2.at[k], r2.at[k], out_send.at[k], out_recv.at[k], {"prompt": source(k)}
                ).start()

    for n in range(count - 1, 0, -1):
        send_out(n)

    for slot, level, row in ((0, 0, chips), (1, 1, chips + 1), (2, 1, chips)):

        def reply(j, carry):
            lanes = lanes_of(j)
            weights = er[slot, :, lanes] * fac[level, row : row + 1, lanes]
            pr[slot, :, lanes] = weights.astype(BF16)
            dr[slot, :, lanes] = (weights * (gr[slot, :, lanes] - inn[level, :, lanes])).astype(BF16)
            return carry

        lax.fori_loop(0, steps, reply, 0, unroll=True)

    send_out(0)
    for c, held in ((0, ((0, 0), (1, 1))), (1, ((2, 1),))):
        rt[c, 0], rt[c, 1] = totals(pr, dr, [(slot, slice(None), level) for slot, level in held])
    pair_r = remote(rt.at[1 - core], rr, pair_send.at[2], pair_recv.at[2], partner)
    pair_r.start()

    kt[...] = kv[0].T
    straight = first // 2 == 0

    def grads_step(j, carry):
        lanes = lanes_of(j)
        parts = []
        for level, slots in enumerate(((0,), (1, 2))):
            gq = dot_nn(kt[:, :prefix_len], dt[level, :, lanes])
            for part, slot in enumerate(slots):
                start = prefix_len + part * own_keys
                gq += dot_nn(kt[:, start : start + own_keys], dr[slot, :, lanes])
            parts.append(gq * scale)
        low = jnp.where(straight, parts[0], parts[1])
        high = jnp.where(straight, parts[1], parts[0])
        for s, value in enumerate((low, high)):
            value = value.T
            for i in range(CHUNK // RBLK):
                spot = pl.multiple_of((j * (CHUNK // RBLK) + i) * 128, 128)
                dq[0, s * RBLK : (s + 1) * RBLK, pl.ds(spot, 128)] = value[
                    i * RBLK : (i + 1) * RBLK
                ]
        return carry

    lax.fori_loop(0, steps, grads_step, 0, unroll=True)

    pair_r.wait_recv()
    rk_out[0] = rt[core, 0] + rr[0]
    rv_out[0] = rt[core, 1] + rr[1]

    total = tb[core, 0] + rb[0]
    for k in range(1, chips):
        remote(
            s2.at[k], r2.at[k], out_send.at[k], out_recv.at[k], {"prompt": target(k)}
        ).wait_recv()
        total = total + r2[k].astype(F32)
    pk_out[...] = total[0]
    pv_out[...] = total[1]

    for k in range(1, chips):
        remote(
            s2.at[k], r2.at[k], out_send.at[k], out_recv.at[k], {"prompt": source(k)}
        ).wait_send()

    @pl.when(core == 1)
    def _():
        for k in range(1, chips):
            remote(
                slot_rows(0), slot_rows(k), gat_send.at[k], gat_recv.at[k], {"prompt": target(k)}
            ).wait_send()
            forward(k).wait_send()

    for copy in list(sums.values()) + [pair_kv, pair_q, pair_r]:
        copy.wait_send()


def finish(*refs):
    *refs, sem = refs
    n = len(refs) // 2
    copies = []
    slots = refs[0].shape[1]
    pieces = slots // RBLK
    for s in range(pieces):
        rows = slice(s * RBLK, (s + 1) * RBLK)
        copies.append(pltpu.make_async_copy(refs[0].at[0, rows], refs[n].at[0, rows], sem.at[s]))
    for i in range(1, n):
        copies.append(pltpu.make_async_copy(refs[i], refs[n + i], sem.at[pieces + i]))
    for copy in copies:
        copy.start()
    for copy in copies:
        copy.wait()


def solution(mesh):
    chips = mesh.shape["prompt"]

    def local(
        queries, grad_out, keys_resp, values_resp, keys_prefix, values_prefix, lengths, block_plan
    ):
        slots, width = queries.shape[1:]
        shard, head = keys_prefix.shape
        heads = width // head
        half = shard // 2
        blocks = slots // RBLK
        own_keys = keys_resp.shape[1]
        prefix = chips * shard
        keys = prefix + 2 * own_keys
        lean = prefix > 1024
        count = chips // (256 // shard)
        vm = pltpu.VMEM
        dma = pltpu.SemaphoreType.DMA
        any_spec = pl.BlockSpec(memory_space=pl.ANY)
        vmem = pl.BlockSpec(memory_space=pltpu.VMEM)
        shapes = (
            (1, slots, width),
            (half, head),
            (half, head),
            (1, own_keys, head),
            (1, own_keys, head),
        )
        parts = pl.pallas_call(
            functools.partial(kernel, chips, heads, lean),
            out_shape=tuple(vm(shape, F32) for shape in shapes),
            in_specs=[any_spec] * 8,
            out_specs=(vmem,) * 5,
            scratch_shapes=[
                pltpu.SMEM(lengths.shape, jnp.int32),
                pltpu.SMEM(block_plan.shape, jnp.int32),
                vm((2, blocks, RBLK, width), BF16),
                vm((2, head, width), BF16),
                vm((2, 2, head, width), BF16),
                vm((2, keys, head), BF16),
                vm((head, keys), BF16),
                vm((2, prefix, width), F32),
                vm((2, 8 if lean else prefix, width), F32),
                vm((2, prefix, width), BF16),
                vm((2, prefix, width), BF16),
                vm((3, own_keys, width), BF16),
                vm((3, own_keys, width), BF16),
                vm((3, own_keys, width), F32),
                vm((3, own_keys, width), F32),
                vm((3, 2, chips + 2, width), F32),
                vm((2, chips + 2, width), F32),
                vm((2, 1, width), F32),
                vm((2, chips, 2, half, head), F32),
                vm((chips, 2, half, head), F32),
                vm((chips, 2, half, head), BF16),
                vm((chips, 2, half, head), BF16),
                vm((2, 2, own_keys, head), F32),
                vm((2, own_keys, head), F32),
                dma((8,)),
                dma((3,)),
                dma((3,)),
                dma((chips,)),
                dma((chips,)),
                dma((chips,)),
                dma((chips,)),
                dma((count,)),
                dma((count,)),
                dma((chips,)),
                dma((chips,)),
            ],
            compiler_params=pltpu.CompilerParams(
                collective_id=0, has_side_effects=True, vmem_limit_bytes=60 * 1024 * 1024
            ),
        )(
            lengths,
            block_plan,
            queries.reshape(blocks, RBLK, width),
            grad_out.reshape(blocks, RBLK, width),
            keys_resp,
            values_resp,
            keys_prefix,
            values_prefix,
        )
        parts = [pltpu.with_memory_space_constraint(part, pltpu.VMEM) for part in parts]
        return pl.pallas_call(
            finish,
            out_shape=tuple(jax.ShapeDtypeStruct(shape, F32) for shape in shapes),
            in_specs=[vmem] * 5,
            out_specs=(any_spec,) * 5,
            scratch_shapes=[dma((blocks + 5,))],
        )(*parts)

    placed = (
        P(("groups", "prompt"), "resp", None),
        P(("groups", "prompt"), "resp", None),
        P(("groups", "prompt"), "resp", None),
        P(("groups", "prompt"), "resp", None),
        P(("groups", "prompt"), None),
        P(("groups", "prompt"), None),
        P(("groups", "prompt")),
        P(("groups", "prompt"), "resp"),
    )
    return jax.shard_map(
        local,
        mesh=mesh,
        in_specs=placed,
        out_specs=(
            P(("groups", "prompt"), "resp", None),
            P(("groups", "prompt", "resp"), None),
            P(("groups", "prompt", "resp"), None),
            P(("groups", "prompt"), "resp", None),
            P(("groups", "prompt"), "resp", None),
        ),
        check_vma=False,
    )
```

```python
import functools
import math

import jax
import jax.numpy as jnp
from jax import lax
from jax.experimental import pallas as pl
from jax.experimental.pallas import tpu as pltpu
from jax.sharding import PartitionSpec as P

RBLK = 128
CHUNK = 256
HIDDEN = -1e30
MESH = pl.DeviceIdType.MESH
F32 = jnp.float32
BF16 = jnp.bfloat16


def remote(src, dst, send_sem, recv_sem, device):
    return pltpu.make_async_remote_copy(
        src_ref=src,
        dst_ref=dst,
        send_sem=send_sem,
        recv_sem=recv_sem,
        device_id=device,
        device_id_type=MESH,
    )


def dot_nt(a, b):
    return lax.dot_general(a, b, (((1,), (1,)), ((), ())), preferred_element_type=F32)


def dot_nn(a, b):
    return lax.dot_general(a, b, (((1,), (0,)), ((), ())), preferred_element_type=F32)


def kernel(
    chips, heads, lean,
    len_hbm, plan_hbm, q_hbm, g_hbm, kr_hbm, vr_hbm, kp_hbm, vp_hbm,
    dq, pk_out, pv_out, rk_out, rv_out,
    len_ref, plan_ref, raw, sb, wk, kv, kt, ep, gp, pt, dt, pr, dr, er, gr, stat, fac, inn,
    tb, rb, s2, r2, rt, rr,
    local_sem, pair_send, pair_recv, gat_send, gat_recv, fwd_send, fwd_recv,
    sum_send, sum_recv, out_send, out_recv,
):
    me = lax.axis_index("prompt")
    core = lax.axis_index("resp")
    partner = {"resp": 1 - core}
    shard = kp_hbm.shape[0]
    half = shard // 2
    prefix_len = chips * shard
    own_keys = kr_hbm.shape[1]
    width = raw.shape[3]
    steps = width // CHUNK
    scale = kv.shape[2] ** (-0.5)
    soft = scale * math.log2(math.e)
    square = chips & (chips - 1) == 0

    def target(k):
        return lax.bitwise_xor(me, k) if square else lax.rem(me + k, chips)

    def source(k):
        return lax.bitwise_xor(me, k) if square else lax.rem(me + chips - k, chips)

    barrier = pltpu.get_barrier_semaphore()
    for k in range(chips - 1, 0, -1):
        pl.semaphore_signal(barrier, inc=1, device_id={"prompt": target(k)}, device_id_type=MESH)
    pl.semaphore_signal(barrier, inc=1, device_id=partner, device_id_type=MESH)

    own_rows = pl.ds(pl.multiple_of(prefix_len + core * own_keys, own_keys), own_keys)
    loads = [
        pltpu.make_async_copy(len_hbm, len_ref, local_sem.at[0]),
        pltpu.make_async_copy(plan_hbm, plan_ref, local_sem.at[1]),
        pltpu.make_async_copy(q_hbm, raw.at[0], local_sem.at[2]),
        pltpu.make_async_copy(g_hbm, raw.at[1], local_sem.at[3]),
        pltpu.make_async_copy(kr_hbm.at[0], kv.at[0, own_rows], local_sem.at[4]),
        pltpu.make_async_copy(vr_hbm.at[0], kv.at[1, own_rows], local_sem.at[5]),
        pltpu.make_async_copy(kp_hbm, kv.at[0, :shard], local_sem.at[6]),
        pltpu.make_async_copy(vp_hbm, kv.at[1, :shard], local_sem.at[7]),
    ]
    for load in loads:
        load.start()
    for load in loads:
        load.wait()

    length = len_ref[0]
    first, second = plan_ref[0, 0], plan_ref[0, 1]
    own_block = jnp.where(first // 2 == core, first, second)
    other_block = jnp.where(first // 2 == core, second, first)
    own_local = lax.rem(own_block, 2)
    sent_local = 1 - own_local
    sent_block = 2 * core + sent_local
    blocks_of = (
        jnp.where(core == 0, own_block, other_block),
        jnp.where(core == 0, other_block, own_block),
    )
    place_of = (core, 1 - core)

    def stack(block_local, block, put):
        rows = lax.broadcasted_iota(jnp.int32, (RBLK, 128), 0) + block * RBLK
        live = rows < length
        for h in range(heads):
            lanes = slice(h * 128, (h + 1) * 128)
            put[0, :, lanes] = raw[0, block_local, :, lanes].T
            grads = raw[1, block_local, :, lanes]
            put[1, :, lanes] = jnp.where(live, grads, jnp.zeros_like(grads)).T

    def lanes_of(j):
        return pl.ds(pl.multiple_of(j * CHUNK, CHUNK), CHUNK)

    def eighths(x):
        return x.reshape(x.shape[0] // 8, 8, x.shape[1])

    def partial(level, row, lanes, scores, gw):
        scores, gw = eighths(scores), eighths(gw)
        top = jnp.max(scores, 0)
        e = jnp.exp2((scores - top) * soft)
        rows = slice(row * 8, row * 8 + 8)
        stat[0, level, rows, lanes] = top
        stat[1, level, rows, lanes] = jnp.sum(e, 0)
        stat[2, level, rows, lanes] = jnp.sum(e * gw, 0)
        return e.reshape(-1, e.shape[2])

    def piece(place, level, block, part, slot, row):
        keys = pl.ds(pl.multiple_of(prefix_len + part * own_keys, own_keys), own_keys)

        def step(j, carry):
            lanes = lanes_of(j)
            lane = lax.broadcasted_iota(jnp.int32, (1, CHUNK), 1)
            limit = jnp.minimum(block * RBLK + lax.rem(lane, RBLK), length - 1)
            spot = lax.broadcasted_iota(jnp.int32, (own_keys, CHUNK), 0) + part * own_keys
            scores = dot_nn(kv[0, keys], wk[place, 0, :, lanes])
            scores = jnp.where(spot <= limit, scores, HIDDEN)
            gw = dot_nn(kv[1, keys], wk[place, 1, :, lanes])
            er[slot, :, lanes] = partial(level, row, lanes, scores, gw)
            gr[slot, :, lanes] = gw
            return carry

        lax.fori_loop(0, steps, step, 0, unroll=True)

    def shard_pass(group, place, level):
        low, high, row = group
        keys = slice(low * shard, high * shard)

        def step(j, carry):
            lanes = lanes_of(j)
            scores = dot_nn(kv[0, keys], wk[place, 0, :, lanes])
            gw = dot_nn(kv[1, keys], wk[place, 1, :, lanes])
            ep[level, keys, lanes] = partial(level, row, lanes, scores, gw)
            if not lean:
                gp[level, keys, lanes] = gw
            return carry

        lax.fori_loop(0, steps, step, 0, unroll=True)

    groups = [(0, 1, 0), (1, 2, 1)] + [(k, k + 2, k // 2 + 1) for k in range(2, chips, 2)]
    row_of = [next(row for low, high, row in groups if low <= k < high) for k in range(chips)]
    tail = len(groups)

    stack(sent_local, sent_block, sb)
    stack(own_local, own_block, wk.at[0])
    piece(0, core, own_block, core, 2 * core, tail)
    shard_pass(groups[0], 0, core)

    pl.semaphore_wait(barrier, chips)

    def slot_rows(k):
        return kv.at[:, k * shard : (k + 1) * shard]

    @pl.when(core == 1)
    def _():
        for k in range(chips - 1, 0, -1):
            remote(
                slot_rows(0), slot_rows(k), gat_send.at[k], gat_recv.at[k], {"prompt": target(k)}
            ).start()

    pair_kv = remote(
        kv.at[:, own_rows], kv.at[:, own_rows], pair_send.at[0], pair_recv.at[0], partner
    )
    pair_kv.start()
    pair_q = remote(sb, wk.at[1], pair_send.at[1], pair_recv.at[1], partner)
    pair_q.start()
    pair_kv.wait_recv()
    pair_q.wait_recv()
    piece(1 - core, 1, blocks_of[1], 0, 1, tail + 1)
    piece(1, 1 - core, other_block, 1 - core, 2 * (1 - core), tail)
    shard_pass(groups[0], 1, 1 - core)

    def forward(k):
        return remote(slot_rows(k), slot_rows(k), fwd_send.at[k], fwd_recv.at[k], partner)

    for group in groups[:0:-1]:
        held = range(group[1] - 1, group[0] - 1, -1)

        @pl.when(core == 1)
        def _():
            for k in held:
                remote(
                    slot_rows(k), slot_rows(k), gat_send.at[k], gat_recv.at[k], {"prompt": source(k)}
                ).wait_recv()
                forward(k).start()

        @pl.when(core == 0)
        def _():
            for k in held:
                forward(k).wait_recv()

        for level in range(2):
            shard_pass(group, place_of[level], level)

    for level in range(2):
        rows = slice(0, (tail + 1 + level) * 8)

        def combine(j, carry):
            lanes = lanes_of(j)
            tops = stat[0, level, rows, lanes]
            factors = jnp.exp2((tops - jnp.max(tops, 0, keepdims=True)) * soft)
            inv = 1.0 / jnp.sum(factors * stat[1, level, rows, lanes], 0, keepdims=True)
            inner = jnp.sum(factors * stat[2, level, rows, lanes], 0, keepdims=True) * inv
            fac[level, rows, lanes] = factors * inv
            inn[level, :, lanes] = jnp.broadcast_to(inner, (8, CHUNK))
            return carry

        lax.fori_loop(0, steps, combine, 0, unroll=True)

    def weigh(level, row, lanes, e, gw):
        weights = eighths(e) * fac[level, row * 8 : row * 8 + 8, lanes]
        grads = weights * (eighths(gw) - inn[level, :, lanes])
        return weights.reshape(e.shape).astype(BF16), grads.reshape(e.shape).astype(BF16)

    def scaled(n):
        for level in range(2):
            for k in range(n * per, (n + 1) * per):
                keys = slice(k * shard, (k + 1) * shard)

                def step(j, carry):
                    lanes = lanes_of(j)
                    if lean:
                        gw = dot_nn(kv[1, keys], wk[place_of[level], 1, :, lanes])
                    else:
                        gw = gp[level, keys, lanes]
                    pt[level, keys, lanes], dt[level, keys, lanes] = weigh(
                        level, row_of[k], lanes, ep[level, keys, lanes], gw
                    )
                    return carry

                lax.fori_loop(0, steps, step, 0, unroll=True)

    def totals(weights, grads, items):
        k_sum = v_sum = None
        for i, rows, level in items:
            place = place_of[level]
            k_part = dot_nt(wk[place, 0], grads[i, rows, :])
            v_part = dot_nt(wk[place, 1], weights[i, rows, :])
            k_sum = k_part if k_sum is None else k_sum + k_part
            v_sum = v_part if v_sum is None else v_sum + v_part
        return (k_sum * scale).T, v_sum.T

    per = 256 // shard
    count = chips // per
    sums = {}
    scaled(count - 1)
    for n in range(count - 1, -1, -1):
        if n > 0:
            scaled(n - 1)
        rows = slice(n * 256, (n + 1) * 256)
        k_sum, v_sum = totals(pt, dt, [(level, rows, level) for level in range(2)])
        span = pl.ds(n * per, per)
        for which, value in ((0, k_sum), (1, v_sum)):
            value = value.reshape(per, 2, half, 128)
            for c in range(2):
                tb[c, span, which] = value[:, c]
        sums[n] = remote(
            tb.at[1 - core, span], rb.at[span], sum_send.at[n], sum_recv.at[n], partner
        )
        sums[n].start()

    def send_out(n):
        sums[n].wait_recv()
        span = pl.ds(n * per, per)
        s2[span] = (tb[core, span] + rb[span]).astype(BF16)
        for k in range((n + 1) * per - 1, n * per - 1, -1):
            if k > 0:
                remote(
                    s2.at[k], r2.at[k], out_send.at[k], out_recv.at[k], {"prompt": source(k)}
                ).start()

    for n in range(count - 1, 0, -1):
        send_out(n)

    for slot, level, row in ((0, 0, tail), (1, 1, tail + 1), (2, 1, tail)):

        def reply(j, carry):
            lanes = lanes_of(j)
            pr[slot, :, lanes], dr[slot, :, lanes] = weigh(
                level, row, lanes, er[slot, :, lanes], gr[slot, :, lanes]
            )
            return carry

        lax.fori_loop(0, steps, reply, 0, unroll=True)

    send_out(0)
    for c, held in ((0, ((0, 0), (1, 1))), (1, ((2, 1),))):
        rt[c, 0], rt[c, 1] = totals(pr, dr, [(slot, slice(None), level) for slot, level in held])
    pair_r = remote(rt.at[1 - core], rr, pair_send.at[2], pair_recv.at[2], partner)
    pair_r.start()

    kt[...] = kv[0].T
    straight = first // 2 == 0

    def grads_step(j, carry):
        lanes = lanes_of(j)
        parts = []
        for level, slots in enumerate(((0,), (1, 2))):
            gq = dot_nn(kt[:, :prefix_len], dt[level, :, lanes])
            for part, slot in enumerate(slots):
                start = prefix_len + part * own_keys
                gq += dot_nn(kt[:, start : start + own_keys], dr[slot, :, lanes])
            parts.append(gq * scale)
        low = jnp.where(straight, parts[0], parts[1])
        high = jnp.where(straight, parts[1], parts[0])
        for s, value in enumerate((low, high)):
            value = value.T
            for i in range(CHUNK // RBLK):
                spot = pl.multiple_of((j * (CHUNK // RBLK) + i) * 128, 128)
                dq[0, s * RBLK : (s + 1) * RBLK, pl.ds(spot, 128)] = value[
                    i * RBLK : (i + 1) * RBLK
                ]
        return carry

    lax.fori_loop(0, steps, grads_step, 0, unroll=True)

    pair_r.wait_recv()
    rk_out[0] = rt[core, 0] + rr[0]
    rv_out[0] = rt[core, 1] + rr[1]

    total = tb[core, 0] + rb[0]
    for k in range(1, chips):
        remote(
            s2.at[k], r2.at[k], out_send.at[k], out_recv.at[k], {"prompt": target(k)}
        ).wait_recv()
        total = total + r2[k].astype(F32)
    pk_out[...] = total[0]
    pv_out[...] = total[1]

    for k in range(1, chips):
        remote(
            s2.at[k], r2.at[k], out_send.at[k], out_recv.at[k], {"prompt": source(k)}
        ).wait_send()

    @pl.when(core == 1)
    def _():
        for k in range(1, chips):
            remote(
                slot_rows(0), slot_rows(k), gat_send.at[k], gat_recv.at[k], {"prompt": target(k)}
            ).wait_send()
            forward(k).wait_send()

    for copy in list(sums.values()) + [pair_kv, pair_q, pair_r]:
        copy.wait_send()


def finish(*refs):
    *refs, sem = refs
    n = len(refs) // 2
    copies = []
    slots = refs[0].shape[1]
    pieces = slots // RBLK
    for s in range(pieces):
        rows = slice(s * RBLK, (s + 1) * RBLK)
        copies.append(pltpu.make_async_copy(refs[0].at[0, rows], refs[n].at[0, rows], sem.at[s]))
    for i in range(1, n):
        copies.append(pltpu.make_async_copy(refs[i], refs[n + i], sem.at[pieces + i]))
    for copy in copies:
        copy.start()
    for copy in copies:
        copy.wait()


def solution(mesh):
    chips = mesh.shape["prompt"]

    def local(
        queries, grad_out, keys_resp, values_resp, keys_prefix, values_prefix, lengths, block_plan
    ):
        slots, width = queries.shape[1:]
        shard, head = keys_prefix.shape
        heads = width // head
        half = shard // 2
        blocks = slots // RBLK
        own_keys = keys_resp.shape[1]
        prefix = chips * shard
        keys = prefix + 2 * own_keys
        lean = prefix > 1024
        count = chips // (256 // shard)
        vm = pltpu.VMEM
        dma = pltpu.SemaphoreType.DMA
        any_spec = pl.BlockSpec(memory_space=pl.ANY)
        vmem = pl.BlockSpec(memory_space=pltpu.VMEM)
        shapes = (
            (1, slots, width),
            (half, head),
            (half, head),
            (1, own_keys, head),
            (1, own_keys, head),
        )
        parts = pl.pallas_call(
            functools.partial(kernel, chips, heads, lean),
            out_shape=tuple(vm(shape, F32) for shape in shapes),
            in_specs=[any_spec] * 8,
            out_specs=(vmem,) * 5,
            scratch_shapes=[
                pltpu.SMEM(lengths.shape, jnp.int32),
                pltpu.SMEM(block_plan.shape, jnp.int32),
                vm((2, blocks, RBLK, width), BF16),
                vm((2, head, width), BF16),
                vm((2, 2, head, width), BF16),
                vm((2, keys, head), BF16),
                vm((head, keys), BF16),
                vm((2, prefix, width), F32),
                vm((2, 8 if lean else prefix, width), F32),
                vm((2, prefix, width), BF16),
                vm((2, prefix, width), BF16),
                vm((3, own_keys, width), BF16),
                vm((3, own_keys, width), BF16),
                vm((3, own_keys, width), F32),
                vm((3, own_keys, width), F32),
                vm((3, 2, (chips // 2 + 3) * 8, width), F32),
                vm((2, (chips // 2 + 3) * 8, width), F32),
                vm((2, 8, width), F32),
                vm((2, chips, 2, half, head), F32),
                vm((chips, 2, half, head), F32),
                vm((chips, 2, half, head), BF16),
                vm((chips, 2, half, head), BF16),
                vm((2, 2, own_keys, head), F32),
                vm((2, own_keys, head), F32),
                dma((8,)),
                dma((3,)),
                dma((3,)),
                dma((chips,)),
                dma((chips,)),
                dma((chips,)),
                dma((chips,)),
                dma((count,)),
                dma((count,)),
                dma((chips,)),
                dma((chips,)),
            ],
            compiler_params=pltpu.CompilerParams(
                collective_id=0, has_side_effects=True, vmem_limit_bytes=60 * 1024 * 1024
            ),
        )(
            lengths,
            block_plan,
            queries.reshape(blocks, RBLK, width),
            grad_out.reshape(blocks, RBLK, width),
            keys_resp,
            values_resp,
            keys_prefix,
            values_prefix,
        )
        parts = [pltpu.with_memory_space_constraint(part, pltpu.VMEM) for part in parts]
        return pl.pallas_call(
            finish,
            out_shape=tuple(jax.ShapeDtypeStruct(shape, F32) for shape in shapes),
            in_specs=[vmem] * 5,
            out_specs=(any_spec,) * 5,
            scratch_shapes=[dma((blocks + 5,))],
        )(*parts)

    placed = (
        P(("groups", "prompt"), "resp", None),
        P(("groups", "prompt"), "resp", None),
        P(("groups", "prompt"), "resp", None),
        P(("groups", "prompt"), "resp", None),
        P(("groups", "prompt"), None),
        P(("groups", "prompt"), None),
        P(("groups", "prompt")),
        P(("groups", "prompt"), "resp"),
    )
    return jax.shard_map(
        local,
        mesh=mesh,
        in_specs=placed,
        out_specs=(
            P(("groups", "prompt"), "resp", None),
            P(("groups", "prompt", "resp"), None),
            P(("groups", "prompt", "resp"), None),
            P(("groups", "prompt"), "resp", None),
            P(("groups", "prompt"), "resp", None),
        ),
        check_vma=False,
    )
```

```python
import functools
import math

import jax
import jax.numpy as jnp
from jax import lax
from jax.experimental import pallas as pl
from jax.experimental.pallas import tpu as pltpu
from jax.sharding import PartitionSpec as P

RBLK = 128
CHUNK = 256
HIDDEN = -1e30
MESH = pl.DeviceIdType.MESH
F32 = jnp.float32
BF16 = jnp.bfloat16


def remote(src, dst, send_sem, recv_sem, device):
    return pltpu.make_async_remote_copy(
        src_ref=src,
        dst_ref=dst,
        send_sem=send_sem,
        recv_sem=recv_sem,
        device_id=device,
        device_id_type=MESH,
    )


def dot_nt(a, b):
    return lax.dot_general(a, b, (((1,), (1,)), ((), ())), preferred_element_type=F32)


def dot_nn(a, b):
    return lax.dot_general(a, b, (((1,), (0,)), ((), ())), preferred_element_type=F32)


def kernel(
    chips, heads, lean,
    len_hbm, plan_hbm, q_hbm, g_hbm, kr_hbm, vr_hbm, kp_hbm, vp_hbm,
    dq, pk_out, pv_out, rk_out, rv_out,
    len_ref, plan_ref, raw, sb, wk, kv, kt, ep, gp, pt, dt, pr, dr, er, gr, stat, fac, inn,
    tb, rb, s2, r2, rt, rr,
    local_sem, pair_send, pair_recv, gat_send, gat_recv, fwd_send, fwd_recv,
    sum_send, sum_recv, out_send, out_recv,
):
    me = lax.axis_index("prompt")
    core = lax.axis_index("resp")
    partner = {"resp": 1 - core}
    shard = kp_hbm.shape[0]
    half = shard // 2
    prefix_len = chips * shard
    own_keys = kr_hbm.shape[1]
    width = raw.shape[3]
    steps = width // CHUNK
    scale = kv.shape[2] ** (-0.5)
    soft = scale * math.log2(math.e)
    square = chips & (chips - 1) == 0

    def target(k):
        return lax.bitwise_xor(me, k) if square else lax.rem(me + k, chips)

    def source(k):
        return lax.bitwise_xor(me, k) if square else lax.rem(me + chips - k, chips)

    near, far = range(chips // 2 - 1, 0, -1), range(chips - 1, chips // 2 - 1, -1)
    barrier = pltpu.get_barrier_semaphore()

    @pl.when(core == 1)
    def _():
        for slots, sender in ((far, 1), (near, 0)):
            for k in slots:
                pl.semaphore_signal(
                    barrier,
                    inc=1,
                    device_id={"prompt": source(k), "resp": sender},
                    device_id_type=MESH,
                )

    pl.semaphore_signal(barrier, inc=1, device_id=partner, device_id_type=MESH)

    own_rows = pl.ds(pl.multiple_of(prefix_len + core * own_keys, own_keys), own_keys)
    loads = [
        pltpu.make_async_copy(len_hbm, len_ref, local_sem.at[0]),
        pltpu.make_async_copy(plan_hbm, plan_ref, local_sem.at[1]),
        pltpu.make_async_copy(q_hbm, raw.at[0], local_sem.at[2]),
        pltpu.make_async_copy(g_hbm, raw.at[1], local_sem.at[3]),
        pltpu.make_async_copy(kr_hbm.at[0], kv.at[0, own_rows], local_sem.at[4]),
        pltpu.make_async_copy(vr_hbm.at[0], kv.at[1, own_rows], local_sem.at[5]),
        pltpu.make_async_copy(kp_hbm, kv.at[0, :shard], local_sem.at[6]),
        pltpu.make_async_copy(vp_hbm, kv.at[1, :shard], local_sem.at[7]),
    ]
    for load in loads:
        load.start()
    for load in loads[6:]:
        load.wait()

    def slot_rows(k):
        return kv.at[:, k * shard : (k + 1) * shard]

    def shard_copy(k):
        return remote(
            slot_rows(0), slot_rows(k), gat_send.at[k], gat_recv.at[k],
            {"prompt": target(k), "resp": 1},
        )

    for sender, slots in ((0, near), (1, far)):

        @pl.when(core == sender)
        def _():
            pl.semaphore_wait(barrier, len(slots) + 1)
            for k in slots:
                shard_copy(k).start()

    for load in loads[:6]:
        load.wait()

    length = len_ref[0]
    first, second = plan_ref[0, 0], plan_ref[0, 1]
    own_block = jnp.where(first // 2 == core, first, second)
    other_block = jnp.where(first // 2 == core, second, first)
    own_local = lax.rem(own_block, 2)
    sent_local = 1 - own_local
    sent_block = 2 * core + sent_local
    blocks_of = (
        jnp.where(core == 0, own_block, other_block),
        jnp.where(core == 0, other_block, own_block),
    )
    place_of = (core, 1 - core)

    def stack(block_local, block, put):
        rows = lax.broadcasted_iota(jnp.int32, (RBLK, 128), 0) + block * RBLK
        live = rows < length
        for h in range(heads):
            lanes = slice(h * 128, (h + 1) * 128)
            put[0, :, lanes] = raw[0, block_local, :, lanes].T
            grads = raw[1, block_local, :, lanes]
            put[1, :, lanes] = jnp.where(live, grads, jnp.zeros_like(grads)).T

    def lanes_of(j):
        return pl.ds(pl.multiple_of(j * CHUNK, CHUNK), CHUNK)

    def eighths(x):
        return x.reshape(x.shape[0] // 8, 8, x.shape[1])

    def partial(level, row, lanes, scores, gw):
        scores, gw = eighths(scores), eighths(gw)
        top = jnp.max(scores, 0)
        e = jnp.exp2((scores - top) * soft)
        rows = slice(row * 8, row * 8 + 8)
        stat[0, level, rows, lanes] = top
        stat[1, level, rows, lanes] = jnp.sum(e, 0)
        stat[2, level, rows, lanes] = jnp.sum(e * gw, 0)
        return e.reshape(-1, e.shape[2])

    def piece(place, level, block, part, slot, row):
        keys = pl.ds(pl.multiple_of(prefix_len + part * own_keys, own_keys), own_keys)

        def step(j, carry):
            lanes = lanes_of(j)
            lane = lax.broadcasted_iota(jnp.int32, (1, CHUNK), 1)
            limit = jnp.minimum(block * RBLK + lax.rem(lane, RBLK), length - 1)
            spot = lax.broadcasted_iota(jnp.int32, (own_keys, CHUNK), 0) + part * own_keys
            scores = dot_nn(kv[0, keys], wk[place, 0, :, lanes])
            scores = jnp.where(spot <= limit, scores, HIDDEN)
            gw = dot_nn(kv[1, keys], wk[place, 1, :, lanes])
            er[slot, :, lanes] = partial(level, row, lanes, scores, gw)
            gr[slot, :, lanes] = gw
            return carry

        lax.fori_loop(0, steps, step, 0, unroll=True)

    def shard_pass(group, place, level):
        low, high, row = group
        keys = slice(low * shard, high * shard)

        def step(j, carry):
            lanes = lanes_of(j)
            scores = dot_nn(kv[0, keys], wk[place, 0, :, lanes])
            gw = dot_nn(kv[1, keys], wk[place, 1, :, lanes])
            ep[level, keys, lanes] = partial(level, row, lanes, scores, gw)
            if not lean:
                gp[level, keys, lanes] = gw
            return carry

        lax.fori_loop(0, steps, step, 0, unroll=True)

    groups = [(0, 1, 0), (1, 2, 1)] + [(k, k + 2, k // 2 + 1) for k in range(2, chips, 2)]
    row_of = [next(row for low, high, row in groups if low <= k < high) for k in range(chips)]
    tail = len(groups)

    stack(sent_local, sent_block, sb)
    pair_q = remote(sb, wk.at[1], pair_send.at[1], pair_recv.at[1], partner)
    pair_q.start()
    pair_kv = remote(
        kv.at[:, own_rows], kv.at[:, own_rows], pair_send.at[0], pair_recv.at[0], partner
    )
    pair_kv.start()
    stack(own_local, own_block, wk.at[0])
    piece(0, core, own_block, core, 2 * core, tail)
    shard_pass(groups[0], 0, core)


    pair_kv.wait_recv()
    pair_q.wait_recv()
    piece(1 - core, 1, blocks_of[1], 0, 1, tail + 1)
    piece(1, 1 - core, other_block, 1 - core, 2 * (1 - core), tail)
    shard_pass(groups[0], 1, 1 - core)

    def forward(k):
        return remote(slot_rows(k), slot_rows(k), fwd_send.at[k], fwd_recv.at[k], partner)

    coming = groups[1 : len(groups) // 2 + 1] + groups[: len(groups) // 2 : -1]
    for i, group in enumerate(coming):
        batch = [group] if i < len(groups) // 2 else coming[i:] if i == len(groups) // 2 else []

        @pl.when(core == 1)
        def _():
            for low, high, _ in batch:
                for k in range(high - 1, low - 1, -1):
                    shard_copy(k).wait_recv()
                    forward(k).start()

        @pl.when(core == 0)
        def _():
            for k in range(group[1] - 1, group[0] - 1, -1):
                forward(k).wait_recv()

        for level in range(2):
            shard_pass(group, place_of[level], level)

    for level in range(2):
        rows = slice(0, (tail + 1 + level) * 8)

        def combine(j, carry):
            lanes = lanes_of(j)
            tops = stat[0, level, rows, lanes]
            factors = jnp.exp2((tops - jnp.max(tops, 0, keepdims=True)) * soft)
            inv = 1.0 / jnp.sum(factors * stat[1, level, rows, lanes], 0, keepdims=True)
            inner = jnp.sum(factors * stat[2, level, rows, lanes], 0, keepdims=True) * inv
            fac[level, rows, lanes] = factors * inv
            inn[level, :, lanes] = jnp.broadcast_to(inner, (8, CHUNK))
            return carry

        lax.fori_loop(0, steps, combine, 0, unroll=True)

    def weigh(level, row, lanes, e, gw):
        weights = eighths(e) * fac[level, row * 8 : row * 8 + 8, lanes]
        grads = weights * (eighths(gw) - inn[level, :, lanes])
        return weights.reshape(e.shape).astype(BF16), grads.reshape(e.shape).astype(BF16)

    def scaled(n):
        for level in range(2):
            for k in range(n * per, (n + 1) * per):
                keys = slice(k * shard, (k + 1) * shard)

                def step(j, carry):
                    lanes = lanes_of(j)
                    if lean:
                        gw = dot_nn(kv[1, keys], wk[place_of[level], 1, :, lanes])
                    else:
                        gw = gp[level, keys, lanes]
                    pt[level, keys, lanes], dt[level, keys, lanes] = weigh(
                        level, row_of[k], lanes, ep[level, keys, lanes], gw
                    )
                    return carry

                lax.fori_loop(0, steps, step, 0, unroll=True)

    def totals(weights, grads, items):
        k_sum = v_sum = None
        for i, rows, level in items:
            place = place_of[level]
            k_part = dot_nt(wk[place, 0], grads[i, rows, :])
            v_part = dot_nt(wk[place, 1], weights[i, rows, :])
            k_sum = k_part if k_sum is None else k_sum + k_part
            v_sum = v_part if v_sum is None else v_sum + v_part
        return (k_sum * scale).T, v_sum.T

    per = 256 // shard
    count = chips // per
    sums = {}

    def send_out(n):
        sums[n].wait_recv()
        span = pl.ds(n * per, per)
        s2[span] = (tb[core, span] + rb[span]).astype(BF16)
        for k in range((n + 1) * per - 1, n * per - 1, -1):
            if k > 0:
                remote(
                    s2.at[k], r2.at[k], out_send.at[k], out_recv.at[k], {"prompt": source(k)}
                ).start()

    for n in range(count - 1, -1, -1):
        scaled(n)
        rows = slice(n * 256, (n + 1) * 256)
        k_sum, v_sum = totals(pt, dt, [(level, rows, level) for level in range(2)])
        span = pl.ds(n * per, per)
        for which, value in ((0, k_sum), (1, v_sum)):
            value = value.reshape(per, 2, half, 128)
            for c in range(2):
                tb[c, span, which] = value[:, c]
        sums[n] = remote(
            tb.at[1 - core, span], rb.at[span], sum_send.at[n], sum_recv.at[n], partner
        )
        sums[n].start()

        @pl.when(core == 0)
        def _():
            send_out(n)


    for slot, level, row in ((0, 0, tail), (1, 1, tail + 1), (2, 1, tail)):

        def reply(j, carry):
            lanes = lanes_of(j)
            pr[slot, :, lanes], dr[slot, :, lanes] = weigh(
                level, row, lanes, er[slot, :, lanes], gr[slot, :, lanes]
            )
            return carry

        lax.fori_loop(0, steps, reply, 0, unroll=True)

    @pl.when(core == 1)
    def _():
        for n in range(count - 1, -1, -1):
            send_out(n)

    for c, held in ((0, ((0, 0), (1, 1))), (1, ((2, 1),))):
        rt[c, 0], rt[c, 1] = totals(pr, dr, [(slot, slice(None), level) for slot, level in held])
    pair_r = remote(rt.at[1 - core], rr, pair_send.at[2], pair_recv.at[2], partner)
    pair_r.start()

    kt[...] = kv[0].T
    straight = first // 2 == 0

    def grads_step(j, carry):
        lanes = lanes_of(j)
        parts = []
        for level, slots in enumerate(((0,), (1, 2))):
            gq = dot_nn(kt[:, :prefix_len], dt[level, :, lanes])
            for part, slot in enumerate(slots):
                start = prefix_len + part * own_keys
                gq += dot_nn(kt[:, start : start + own_keys], dr[slot, :, lanes])
            parts.append(gq * scale)
        low = jnp.where(straight, parts[0], parts[1])
        high = jnp.where(straight, parts[1], parts[0])
        for s, value in enumerate((low, high)):
            value = value.T
            for i in range(CHUNK // RBLK):
                spot = pl.multiple_of((j * (CHUNK // RBLK) + i) * 128, 128)
                dq[0, s * RBLK : (s + 1) * RBLK, pl.ds(spot, 128)] = value[
                    i * RBLK : (i + 1) * RBLK
                ]
        return carry

    lax.fori_loop(0, steps, grads_step, 0, unroll=True)

    pair_r.wait_recv()
    rk_out[0] = rt[core, 0] + rr[0]
    rv_out[0] = rt[core, 1] + rr[1]

    total = tb[core, 0] + rb[0]
    for k in range(1, chips):
        remote(
            s2.at[k], r2.at[k], out_send.at[k], out_recv.at[k], {"prompt": target(k)}
        ).wait_recv()
        total = total + r2[k].astype(F32)
    pk_out[...] = total[0]
    pv_out[...] = total[1]

    for k in range(1, chips):
        remote(
            s2.at[k], r2.at[k], out_send.at[k], out_recv.at[k], {"prompt": source(k)}
        ).wait_send()

    for sender, slots in ((0, near), (1, far)):

        @pl.when(core == sender)
        def _():
            for k in slots:
                shard_copy(k).wait_send()

    @pl.when(core == 1)
    def _():
        for k in range(1, chips):
            forward(k).wait_send()

    for copy in list(sums.values()) + [pair_kv, pair_q, pair_r]:
        copy.wait_send()


def finish(*refs):
    *refs, sem = refs
    n = len(refs) // 2
    copies = []
    slots = refs[0].shape[1]
    pieces = slots // RBLK
    for s in range(pieces):
        rows = slice(s * RBLK, (s + 1) * RBLK)
        copies.append(pltpu.make_async_copy(refs[0].at[0, rows], refs[n].at[0, rows], sem.at[s]))
    for i in range(1, n):
        copies.append(pltpu.make_async_copy(refs[i], refs[n + i], sem.at[pieces + i]))
    for copy in copies:
        copy.start()
    for copy in copies:
        copy.wait()


def solution(mesh):
    chips = mesh.shape["prompt"]

    def local(
        queries, grad_out, keys_resp, values_resp, keys_prefix, values_prefix, lengths, block_plan
    ):
        slots, width = queries.shape[1:]
        shard, head = keys_prefix.shape
        heads = width // head
        half = shard // 2
        blocks = slots // RBLK
        own_keys = keys_resp.shape[1]
        prefix = chips * shard
        keys = prefix + 2 * own_keys
        lean = prefix > 1024
        count = chips // (256 // shard)
        vm = pltpu.VMEM
        dma = pltpu.SemaphoreType.DMA
        any_spec = pl.BlockSpec(memory_space=pl.ANY)
        vmem = pl.BlockSpec(memory_space=pltpu.VMEM)
        shapes = (
            (1, slots, width),
            (half, head),
            (half, head),
            (1, own_keys, head),
            (1, own_keys, head),
        )
        parts = pl.pallas_call(
            functools.partial(kernel, chips, heads, lean),
            out_shape=tuple(vm(shape, F32) for shape in shapes),
            in_specs=[any_spec] * 8,
            out_specs=(vmem,) * 5,
            scratch_shapes=[
                pltpu.SMEM(lengths.shape, jnp.int32),
                pltpu.SMEM(block_plan.shape, jnp.int32),
                vm((2, blocks, RBLK, width), BF16),
                vm((2, head, width), BF16),
                vm((2, 2, head, width), BF16),
                vm((2, keys, head), BF16),
                vm((head, keys), BF16),
                vm((2, prefix, width), F32),
                vm((2, 8 if lean else prefix, width), F32),
                vm((2, prefix, width), BF16),
                vm((2, prefix, width), BF16),
                vm((3, own_keys, width), BF16),
                vm((3, own_keys, width), BF16),
                vm((3, own_keys, width), F32),
                vm((3, own_keys, width), F32),
                vm((3, 2, (chips // 2 + 3) * 8, width), F32),
                vm((2, (chips // 2 + 3) * 8, width), F32),
                vm((2, 8, width), F32),
                vm((2, chips, 2, half, head), F32),
                vm((chips, 2, half, head), F32),
                vm((chips, 2, half, head), BF16),
                vm((chips, 2, half, head), BF16),
                vm((2, 2, own_keys, head), F32),
                vm((2, own_keys, head), F32),
                dma((8,)),
                dma((3,)),
                dma((3,)),
                dma((chips,)),
                dma((chips,)),
                dma((chips,)),
                dma((chips,)),
                dma((count,)),
                dma((count,)),
                dma((chips,)),
                dma((chips,)),
            ],
            compiler_params=pltpu.CompilerParams(
                collective_id=0, has_side_effects=True, vmem_limit_bytes=60 * 1024 * 1024
            ),
        )(
            lengths,
            block_plan,
            queries.reshape(blocks, RBLK, width),
            grad_out.reshape(blocks, RBLK, width),
            keys_resp,
            values_resp,
            keys_prefix,
            values_prefix,
        )
        parts = [pltpu.with_memory_space_constraint(part, pltpu.VMEM) for part in parts]
        return pl.pallas_call(
            finish,
            out_shape=tuple(jax.ShapeDtypeStruct(shape, F32) for shape in shapes),
            in_specs=[vmem] * 5,
            out_specs=(any_spec,) * 5,
            scratch_shapes=[dma((blocks + 5,))],
        )(*parts)

    placed = (
        P(("groups", "prompt"), "resp", None),
        P(("groups", "prompt"), "resp", None),
        P(("groups", "prompt"), "resp", None),
        P(("groups", "prompt"), "resp", None),
        P(("groups", "prompt"), None),
        P(("groups", "prompt"), None),
        P(("groups", "prompt")),
        P(("groups", "prompt"), "resp"),
    )
    return jax.shard_map(
        local,
        mesh=mesh,
        in_specs=placed,
        out_specs=(
            P(("groups", "prompt"), "resp", None),
            P(("groups", "prompt", "resp"), None),
            P(("groups", "prompt", "resp"), None),
            P(("groups", "prompt"), "resp", None),
            P(("groups", "prompt"), "resp", None),
        ),
        check_vma=False,
    )
```

```python
import functools
import math

import jax
import jax.numpy as jnp
from jax import lax
from jax.experimental import pallas as pl
from jax.experimental.pallas import tpu as pltpu
from jax.sharding import PartitionSpec as P

RBLK = 128
CHUNK = 256
HIDDEN = -1e30
MESH = pl.DeviceIdType.MESH
F32 = jnp.float32
BF16 = jnp.bfloat16


def remote(src, dst, send_sem, recv_sem, device):
    return pltpu.make_async_remote_copy(
        src_ref=src,
        dst_ref=dst,
        send_sem=send_sem,
        recv_sem=recv_sem,
        device_id=device,
        device_id_type=MESH,
    )


def dot_nt(a, b):
    return lax.dot_general(a, b, (((1,), (1,)), ((), ())), preferred_element_type=F32)


def dot_nn(a, b):
    return lax.dot_general(a, b, (((1,), (0,)), ((), ())), preferred_element_type=F32)


def kernel(
    chips, heads, lean,
    len_hbm, plan_hbm, q_hbm, g_hbm, kr_hbm, vr_hbm, kp_hbm, vp_hbm,
    dq, pk_out, pv_out, rk_out, rv_out,
    len_ref, plan_ref, raw, sb, wk, kv, kt, ep, gp, pt, dt, pr, dr, er, gr, stat, fac, inn,
    tb, rb, s2, r2, rt, rr,
    local_sem, pair_send, pair_recv, gat_send, gat_recv, fwd_send, fwd_recv,
    sum_send, sum_recv, out_send, out_recv,
):
    me = lax.axis_index("prompt")
    core = lax.axis_index("resp")
    partner = {"resp": 1 - core}
    shard = kp_hbm.shape[0]
    half = shard // 2
    prefix_len = chips * shard
    own_keys = kr_hbm.shape[1]
    width = raw.shape[3]
    steps = width // CHUNK
    scale = kv.shape[2] ** (-0.5)
    soft = scale * math.log2(math.e)
    square = chips & (chips - 1) == 0

    def target(k):
        return lax.bitwise_xor(me, k) if square else lax.rem(me + k, chips)

    def source(k):
        return lax.bitwise_xor(me, k) if square else lax.rem(me + chips - k, chips)

    near, far = range(chips // 2 - 1, 0, -1), range(chips - 1, chips // 2 - 1, -1)
    barrier = pltpu.get_barrier_semaphore()

    @pl.when(core == 1)
    def _():
        for slots, sender in ((far, 1), (near, 0)):
            for k in slots:
                pl.semaphore_signal(
                    barrier,
                    inc=1,
                    device_id={"prompt": source(k), "resp": sender},
                    device_id_type=MESH,
                )

    pl.semaphore_signal(barrier, inc=1, device_id=partner, device_id_type=MESH)

    own_rows = pl.ds(pl.multiple_of(prefix_len + core * own_keys, own_keys), own_keys)
    def load(sem, *pairs):
        for src, dst in pairs:
            pltpu.make_async_copy(src, dst, local_sem.at[sem]).start()

    def loaded(sem, whole):
        pltpu.make_async_copy(whole, whole, local_sem.at[sem]).wait()

    load(0, (kp_hbm, kv.at[0, :shard]), (vp_hbm, kv.at[1, :shard]))
    load(1, (q_hbm, raw.at[0]), (g_hbm, raw.at[1]))
    load(2, (len_hbm, len_ref))
    load(3, (plan_hbm, plan_ref))
    load(4, (kr_hbm.at[0], kv.at[0, own_rows]), (vr_hbm.at[0], kv.at[1, own_rows]))
    loaded(0, kv.at[:, :shard])

    groups = [(0, 1, 0), (1, 2, 1)] + [(k, k + 2, k // 2 + 1) for k in range(2, chips, 2)]
    row_of = [next(row for low, high, row in groups if low <= k < high) for k in range(chips)]
    tail = len(groups)

    def slot_rows(low, high):
        return kv.at[:, low * shard : high * shard]

    def shard_copy(k):
        return remote(
            slot_rows(0, 1), slot_rows(k, k + 1), gat_send.at[0], gat_recv.at[row_of[k]],
            {"prompt": target(k), "resp": 1},
        )

    def shards_done(low, high):
        rows = slot_rows(low, high)
        return remote(rows, rows, gat_send.at[0], gat_recv.at[row_of[low]], partner)

    for sender, slots in ((0, near), (1, far)):

        @pl.when(core == sender)
        def _():
            pl.semaphore_wait(barrier, len(slots) + 1)
            for k in slots:
                shard_copy(k).start()

    loaded(1, raw)
    loaded(2, len_ref)
    loaded(3, plan_ref)
    loaded(4, kv.at[:, own_rows])

    length = len_ref[0]
    first, second = plan_ref[0, 0], plan_ref[0, 1]
    own_block = jnp.where(first // 2 == core, first, second)
    other_block = jnp.where(first // 2 == core, second, first)
    own_local = lax.rem(own_block, 2)
    sent_local = 1 - own_local
    sent_block = 2 * core + sent_local
    blocks_of = (
        jnp.where(core == 0, own_block, other_block),
        jnp.where(core == 0, other_block, own_block),
    )
    place_of = (core, 1 - core)

    def stack(block_local, block, put):
        rows = lax.broadcasted_iota(jnp.int32, (RBLK, 128), 0) + block * RBLK
        live = rows < length
        for h in range(heads):
            lanes = slice(h * 128, (h + 1) * 128)
            put[0, :, lanes] = raw[0, block_local, :, lanes].T
            grads = raw[1, block_local, :, lanes]
            put[1, :, lanes] = jnp.where(live, grads, jnp.zeros_like(grads)).T

    def lanes_of(j):
        return pl.ds(pl.multiple_of(j * CHUNK, CHUNK), CHUNK)

    def eighths(x):
        return x.reshape(x.shape[0] // 8, 8, x.shape[1])

    def partial(level, row, lanes, scores, gw):
        scores, gw = eighths(scores), eighths(gw)
        top = jnp.max(scores, 0)
        e = jnp.exp2((scores - top) * soft)
        rows = slice(row * 8, row * 8 + 8)
        stat[0, level, rows, lanes] = top
        stat[1, level, rows, lanes] = jnp.sum(e, 0)
        stat[2, level, rows, lanes] = jnp.sum(e * gw, 0)
        return e.reshape(-1, e.shape[2])

    def piece(place, level, block, part, slot, row):
        keys = pl.ds(pl.multiple_of(prefix_len + part * own_keys, own_keys), own_keys)

        def step(j, carry):
            lanes = lanes_of(j)
            lane = lax.broadcasted_iota(jnp.int32, (1, CHUNK), 1)
            limit = jnp.minimum(block * RBLK + lax.rem(lane, RBLK), length - 1)
            spot = lax.broadcasted_iota(jnp.int32, (own_keys, CHUNK), 0) + part * own_keys
            scores = dot_nn(kv[0, keys], wk[place, 0, :, lanes])
            scores = jnp.where(spot <= limit, scores, HIDDEN)
            gw = dot_nn(kv[1, keys], wk[place, 1, :, lanes])
            er[slot, :, lanes] = partial(level, row, lanes, scores, gw)
            gr[slot, :, lanes] = gw
            return carry

        lax.fori_loop(0, steps, step, 0, unroll=True)

    def shard_pass(group, place, level):
        low, high, row = group
        keys = slice(low * shard, high * shard)

        def step(j, carry):
            lanes = pl.ds(pl.multiple_of(j * 2 * CHUNK, CHUNK), 2 * CHUNK)
            scores = dot_nn(kv[0, keys], wk[place, 0, :, lanes])
            gw = dot_nn(kv[1, keys], wk[place, 1, :, lanes])
            ep[level, keys, lanes] = partial(level, row, lanes, scores, gw)
            if not lean:
                gp[level, keys, lanes] = gw
            return carry

        lax.fori_loop(0, steps // 2, step, 0, unroll=True)

    stack(sent_local, sent_block, sb)
    pair_q = remote(sb, wk.at[1], pair_send.at[1], pair_recv.at[1], partner)
    pair_q.start()
    pair_kv = remote(
        kv.at[:, own_rows], kv.at[:, own_rows], pair_send.at[0], pair_recv.at[0], partner
    )
    pair_kv.start()
    stack(own_local, own_block, wk.at[0])
    piece(0, core, own_block, core, 2 * core, tail)
    shard_pass(groups[0], 0, core)


    pair_kv.wait_recv()
    pair_q.wait_recv()
    piece(1 - core, 1, blocks_of[1], 0, 1, tail + 1)
    piece(1, 1 - core, other_block, 1 - core, 2 * (1 - core), tail)
    shard_pass(groups[0], 1, 1 - core)

    def forward(low, high):
        rows = slot_rows(low, high)
        return remote(rows, rows, fwd_send.at[0], fwd_recv.at[row_of[low]], partner)

    coming = groups[1 : len(groups) // 2 + 1] + groups[: len(groups) // 2 : -1]
    for i, group in enumerate(coming):
        batch = [group]

        @pl.when(core == 1)
        def _():
            for low, high, _ in batch:
                shards_done(low, high).wait_recv()
                forward(low, high).start()

        @pl.when(core == 0)
        def _():
            forward(*group[:2]).wait_recv()

        for level in range(2):
            shard_pass(group, place_of[level], level)

    for level in range(2):
        rows = slice(0, (tail + 1 + level) * 8)

        def combine(j, carry):
            lanes = lanes_of(j)
            tops = stat[0, level, rows, lanes]
            factors = jnp.exp2((tops - jnp.max(tops, 0, keepdims=True)) * soft)
            inv = 1.0 / jnp.sum(factors * stat[1, level, rows, lanes], 0, keepdims=True)
            inner = jnp.sum(factors * stat[2, level, rows, lanes], 0, keepdims=True) * inv
            fac[level, rows, lanes] = factors * inv
            inn[level, :, lanes] = jnp.broadcast_to(inner, (8, CHUNK))
            return carry

        lax.fori_loop(0, steps, combine, 0, unroll=True)

    def weigh(level, row, lanes, e, gw):
        weights = eighths(e) * fac[level, row * 8 : row * 8 + 8, lanes]
        grads = weights * (eighths(gw) - inn[level, :, lanes])
        return weights.reshape(e.shape).astype(BF16), grads.reshape(e.shape).astype(BF16)

    def scaled(n):
        for level in range(2):
            for k in range(n * per, (n + 1) * per):
                keys = slice(k * shard, (k + 1) * shard)

                def step(j, carry):
                    lanes = lanes_of(j)
                    if lean:
                        gw = dot_nn(kv[1, keys], wk[place_of[level], 1, :, lanes])
                    else:
                        gw = gp[level, keys, lanes]
                    pt[level, keys, lanes], dt[level, keys, lanes] = weigh(
                        level, row_of[k], lanes, ep[level, keys, lanes], gw
                    )
                    return carry

                lax.fori_loop(0, steps, step, 0, unroll=True)

    def totals(weights, grads, items):
        k_sum = v_sum = None
        for i, rows, level in items:
            place = place_of[level]
            k_part = dot_nt(wk[place, 0], grads[i, rows, :])
            v_part = dot_nt(wk[place, 1], weights[i, rows, :])
            k_sum = k_part if k_sum is None else k_sum + k_part
            v_sum = v_part if v_sum is None else v_sum + v_part
        return (k_sum * scale).T, v_sum.T

    per = 256 // shard
    count = chips // per
    sums = {}

    def send_out(n):
        sums[n].wait_recv()
        span = pl.ds(n * per, per)
        s2[span] = (tb[core, span] + rb[span]).astype(BF16)
        for k in range((n + 1) * per - 1, n * per - 1, -1):
            if k > 0:
                remote(
                    s2.at[k], r2.at[k], out_send.at[0], out_recv.at[0], {"prompt": source(k)}
                ).start()

    for n in range(count - 1, -1, -1):
        scaled(n)
        rows = slice(n * 256, (n + 1) * 256)
        k_sum, v_sum = totals(pt, dt, [(level, rows, level) for level in range(2)])
        span = pl.ds(n * per, per)
        for which, value in ((0, k_sum), (1, v_sum)):
            value = value.reshape(per, 2, half, 128)
            for c in range(2):
                tb[c, span, which] = value[:, c]
        sums[n] = remote(
            tb.at[1 - core, span], rb.at[span], sum_send.at[n], sum_recv.at[n], partner
        )
        sums[n].start()

        @pl.when(core == 0)
        def _():
            send_out(n)


    for slot, level, row in ((0, 0, tail), (1, 1, tail + 1), (2, 1, tail)):

        def reply(j, carry):
            lanes = lanes_of(j)
            pr[slot, :, lanes], dr[slot, :, lanes] = weigh(
                level, row, lanes, er[slot, :, lanes], gr[slot, :, lanes]
            )
            return carry

        lax.fori_loop(0, steps, reply, 0, unroll=True)

    @pl.when(core == 1)
    def _():
        for n in range(count - 1, -1, -1):
            send_out(n)

    for c, held in ((0, ((0, 0), (1, 1))), (1, ((2, 1),))):
        rt[c, 0], rt[c, 1] = totals(pr, dr, [(slot, slice(None), level) for slot, level in held])
    pair_r = remote(rt.at[1 - core], rr, pair_send.at[2], pair_recv.at[2], partner)
    pair_r.start()

    kt[...] = kv[0].T
    straight = first // 2 == 0

    def grads_step(j, carry):
        lanes = lanes_of(j)
        parts = []
        for level, slots in enumerate(((0,), (1, 2))):
            gq = dot_nn(kt[:, :prefix_len], dt[level, :, lanes])
            for part, slot in enumerate(slots):
                start = prefix_len + part * own_keys
                gq += dot_nn(kt[:, start : start + own_keys], dr[slot, :, lanes])
            parts.append(gq * scale)
        low = jnp.where(straight, parts[0], parts[1])
        high = jnp.where(straight, parts[1], parts[0])
        for s, value in enumerate((low, high)):
            value = value.T
            for i in range(CHUNK // RBLK):
                spot = pl.multiple_of((j * (CHUNK // RBLK) + i) * 128, 128)
                dq[0, s * RBLK : (s + 1) * RBLK, pl.ds(spot, 128)] = value[
                    i * RBLK : (i + 1) * RBLK
                ]
        return carry

    lax.fori_loop(0, steps, grads_step, 0, unroll=True)

    pair_r.wait_recv()
    rk_out[0] = rt[core, 0] + rr[0]
    rv_out[0] = rt[core, 1] + rr[1]

    for sender, slots in ((0, near), (1, far)):

        @pl.when(core == sender)
        def _():
            shards_done(0, len(slots)).wait_send()

    @pl.when(core == 1)
    def _():
        forward(1, chips).wait_send()

    for copy in list(sums.values()) + [pair_kv, pair_q, pair_r]:
        copy.wait_send()

    total = tb[core, 0] + rb[0]
    spread = remote(s2.at[1:chips], r2.at[1:chips], out_send.at[0], out_recv.at[0], partner)
    spread.wait_recv()
    for k in range(1, chips):
        total = total + r2[k].astype(F32)
    pk_out[...] = total[0]
    pv_out[...] = total[1]
    spread.wait_send()


def finish(*refs):
    *refs, sem = refs
    n = len(refs) // 2
    copies = []
    slots = refs[0].shape[1]
    pieces = slots // RBLK
    for s in range(pieces):
        rows = slice(s * RBLK, (s + 1) * RBLK)
        copies.append(pltpu.make_async_copy(refs[0].at[0, rows], refs[n].at[0, rows], sem.at[s]))
    for i in range(1, n):
        copies.append(pltpu.make_async_copy(refs[i], refs[n + i], sem.at[pieces + i]))
    for copy in copies:
        copy.start()
    for copy in copies:
        copy.wait()


def solution(mesh):
    chips = mesh.shape["prompt"]

    def local(
        queries, grad_out, keys_resp, values_resp, keys_prefix, values_prefix, lengths, block_plan
    ):
        slots, width = queries.shape[1:]
        shard, head = keys_prefix.shape
        heads = width // head
        half = shard // 2
        blocks = slots // RBLK
        own_keys = keys_resp.shape[1]
        prefix = chips * shard
        keys = prefix + 2 * own_keys
        lean = prefix > 1024
        count = chips // (256 // shard)
        vm = pltpu.VMEM
        dma = pltpu.SemaphoreType.DMA
        any_spec = pl.BlockSpec(memory_space=pl.ANY)
        vmem = pl.BlockSpec(memory_space=pltpu.VMEM)
        shapes = (
            (1, slots, width),
            (half, head),
            (half, head),
            (1, own_keys, head),
            (1, own_keys, head),
        )
        parts = pl.pallas_call(
            functools.partial(kernel, chips, heads, lean),
            out_shape=tuple(vm(shape, F32) for shape in shapes),
            in_specs=[any_spec] * 8,
            out_specs=(vmem,) * 5,
            scratch_shapes=[
                pltpu.SMEM(lengths.shape, jnp.int32),
                pltpu.SMEM(block_plan.shape, jnp.int32),
                vm((2, blocks, RBLK, width), BF16),
                vm((2, head, width), BF16),
                vm((2, 2, head, width), BF16),
                vm((2, keys, head), BF16),
                vm((head, keys), BF16),
                vm((2, prefix, width), F32),
                vm((2, 8 if lean else prefix, width), F32),
                vm((2, prefix, width), BF16),
                vm((2, prefix, width), BF16),
                vm((3, own_keys, width), BF16),
                vm((3, own_keys, width), BF16),
                vm((3, own_keys, width), F32),
                vm((3, own_keys, width), F32),
                vm((3, 2, (chips // 2 + 3) * 8, width), F32),
                vm((2, (chips // 2 + 3) * 8, width), F32),
                vm((2, 8, width), F32),
                vm((2, chips, 2, half, head), F32),
                vm((chips, 2, half, head), F32),
                vm((chips, 2, half, head), BF16),
                vm((chips, 2, half, head), BF16),
                vm((2, 2, own_keys, head), F32),
                vm((2, own_keys, head), F32),
                dma((5,)),
                dma((3,)),
                dma((3,)),
                dma((1,)),
                dma((chips // 2 + 1,)),
                dma((1,)),
                dma((chips // 2 + 1,)),
                dma((count,)),
                dma((count,)),
                dma((1,)),
                dma((1,)),
            ],
            compiler_params=pltpu.CompilerParams(
                collective_id=0, has_side_effects=True, vmem_limit_bytes=60 * 1024 * 1024
            ),
        )(
            lengths,
            block_plan,
            queries.reshape(blocks, RBLK, width),
            grad_out.reshape(blocks, RBLK, width),
            keys_resp,
            values_resp,
            keys_prefix,
            values_prefix,
        )
        parts = [pltpu.with_memory_space_constraint(part, pltpu.VMEM) for part in parts]
        return pl.pallas_call(
            finish,
            out_shape=tuple(jax.ShapeDtypeStruct(shape, F32) for shape in shapes),
            in_specs=[vmem] * 5,
            out_specs=(any_spec,) * 5,
            scratch_shapes=[dma((blocks + 5,))],
        )(*parts)

    placed = (
        P(("groups", "prompt"), "resp", None),
        P(("groups", "prompt"), "resp", None),
        P(("groups", "prompt"), "resp", None),
        P(("groups", "prompt"), "resp", None),
        P(("groups", "prompt"), None),
        P(("groups", "prompt"), None),
        P(("groups", "prompt")),
        P(("groups", "prompt"), "resp"),
    )
    return jax.shard_map(
        local,
        mesh=mesh,
        in_specs=placed,
        out_specs=(
            P(("groups", "prompt"), "resp", None),
            P(("groups", "prompt", "resp"), None),
            P(("groups", "prompt", "resp"), None),
            P(("groups", "prompt"), "resp", None),
            P(("groups", "prompt"), "resp", None),
        ),
        check_vma=False,
    )
```

```python
import functools
import math

import jax
import jax.numpy as jnp
from jax import lax
from jax.experimental import pallas as pl
from jax.experimental.pallas import tpu as pltpu
from jax.sharding import PartitionSpec as P

RBLK = 128
CHUNK = 256
HIDDEN = -1e30
MESH = pl.DeviceIdType.MESH
F32 = jnp.float32
BF16 = jnp.bfloat16


def remote(src, dst, send_sem, recv_sem, device):
    return pltpu.make_async_remote_copy(
        src_ref=src,
        dst_ref=dst,
        send_sem=send_sem,
        recv_sem=recv_sem,
        device_id=device,
        device_id_type=MESH,
    )


def dot_nt(a, b):
    return lax.dot_general(a, b, (((1,), (1,)), ((), ())), preferred_element_type=F32)


def dot_nn(a, b):
    return lax.dot_general(a, b, (((1,), (0,)), ((), ())), preferred_element_type=F32)


def kernel(
    chips, heads, lean,
    len_hbm, plan_hbm, q_hbm, g_hbm, kr_hbm, vr_hbm, kp_hbm, vp_hbm,
    dq, pk_out, pv_out, rk_out, rv_out,
    len_ref, plan_ref, raw, sb, wk, kv, kt, ep, gp, pt, dt, pr, dr, er, gr, stat, fac, inn,
    tb, rb, s2, r2, rt, rr,
    local_sem, pair_send, pair_recv, gat_send, gat_recv, fwd_send, fwd_recv,
    sum_send, sum_recv, out_send, out_recv,
):
    me = lax.axis_index("prompt")
    core = lax.axis_index("resp")
    partner = {"resp": 1 - core}
    shard = kp_hbm.shape[0]
    half = shard // 2
    prefix_len = chips * shard
    own_keys = kr_hbm.shape[1]
    width = raw.shape[3]
    steps = width // CHUNK
    scale = kv.shape[2] ** (-0.5)
    soft = scale * math.log2(math.e)
    square = chips & (chips - 1) == 0

    def target(k):
        return lax.bitwise_xor(me, k) if square else lax.rem(me + k, chips)

    def source(k):
        return lax.bitwise_xor(me, k) if square else lax.rem(me + chips - k, chips)

    near, far = range(chips // 2 - 1, 0, -1), range(chips - 1, chips // 2 - 1, -1)
    barrier = pltpu.get_barrier_semaphore()

    @pl.when(core == 1)
    def _():
        for slots, sender in ((far, 1), (near, 0)):
            for k in slots:
                pl.semaphore_signal(
                    barrier,
                    inc=1,
                    device_id={"prompt": source(k), "resp": sender},
                    device_id_type=MESH,
                )

    pl.semaphore_signal(barrier, inc=1, device_id=partner, device_id_type=MESH)

    own_rows = pl.ds(pl.multiple_of(prefix_len + core * own_keys, own_keys), own_keys)
    def load(sem, *pairs):
        for src, dst in pairs:
            pltpu.make_async_copy(src, dst, local_sem.at[sem]).start()

    def loaded(sem, whole):
        pltpu.make_async_copy(whole, whole, local_sem.at[sem]).wait()

    load(0, (kp_hbm, kv.at[0, :shard]), (vp_hbm, kv.at[1, :shard]))
    load(1, (q_hbm, raw.at[0]), (g_hbm, raw.at[1]))
    load(2, (len_hbm, len_ref))
    load(3, (plan_hbm, plan_ref))
    load(4, (kr_hbm.at[0], kv.at[0, own_rows]), (vr_hbm.at[0], kv.at[1, own_rows]))
    loaded(0, kv.at[:, :shard])

    groups = [(0, 1, 0), (1, 2, 1)] + [(k, k + 2, k // 2 + 1) for k in range(2, chips, 2)]
    row_of = [next(row for low, high, row in groups if low <= k < high) for k in range(chips)]
    tail = len(groups)

    def slot_rows(low, high):
        return kv.at[:, low * shard : high * shard]

    def shard_copy(k):
        return remote(
            slot_rows(0, 1), slot_rows(k, k + 1), gat_send.at[0], gat_recv.at[row_of[k]],
            {"prompt": target(k), "resp": 1},
        )

    def shards_done(low, high):
        rows = slot_rows(low, high)
        return remote(rows, rows, gat_send.at[0], gat_recv.at[row_of[low]], partner)

    for sender, slots in ((0, near), (1, far)):

        @pl.when(core == sender)
        def _():
            pl.semaphore_wait(barrier, len(slots) + 1)
            for k in slots:
                shard_copy(k).start()

    loaded(1, raw)
    loaded(2, len_ref)
    loaded(3, plan_ref)
    loaded(4, kv.at[:, own_rows])

    length = len_ref[0]
    first, second = plan_ref[0, 0], plan_ref[0, 1]
    own_block = jnp.where(first // 2 == core, first, second)
    other_block = jnp.where(first // 2 == core, second, first)
    own_local = lax.rem(own_block, 2)
    sent_local = 1 - own_local
    sent_block = 2 * core + sent_local
    blocks_of = (
        jnp.where(core == 0, own_block, other_block),
        jnp.where(core == 0, other_block, own_block),
    )
    place_of = (core, 1 - core)

    def stack(block_local, block, put):
        rows = lax.broadcasted_iota(jnp.int32, (RBLK, 128), 0) + block * RBLK
        live = rows < length
        for h in range(heads):
            lanes = slice(h * 128, (h + 1) * 128)
            put[0, :, lanes] = raw[0, block_local, :, lanes].T
            grads = raw[1, block_local, :, lanes]
            put[1, :, lanes] = jnp.where(live, grads, jnp.zeros_like(grads)).T

    def lanes_of(j):
        return pl.ds(pl.multiple_of(j * CHUNK, CHUNK), CHUNK)

    def eighths(x):
        return x.reshape(x.shape[0] // 8, 8, x.shape[1])

    def partial(level, row, lanes, scores, gw):
        scores, gw = eighths(scores), eighths(gw)
        top = jnp.max(scores, 0)
        e = jnp.exp2((scores - top) * soft)
        rows = slice(row * 8, row * 8 + 8)
        stat[0, level, rows, lanes] = top
        stat[1, level, rows, lanes] = jnp.sum(e, 0)
        stat[2, level, rows, lanes] = jnp.sum(e * gw, 0)
        return e.reshape(-1, e.shape[2])

    def piece(place, level, block, part, slot, row):
        keys = pl.ds(pl.multiple_of(prefix_len + part * own_keys, own_keys), own_keys)

        def step(j, carry):
            lanes = lanes_of(j)
            lane = lax.broadcasted_iota(jnp.int32, (1, CHUNK), 1)
            limit = jnp.minimum(block * RBLK + lax.rem(lane, RBLK), length - 1)
            spot = lax.broadcasted_iota(jnp.int32, (own_keys, CHUNK), 0) + part * own_keys
            scores = dot_nn(kv[0, keys], wk[place, 0, :, lanes])
            scores = jnp.where(spot <= limit, scores, HIDDEN)
            gw = dot_nn(kv[1, keys], wk[place, 1, :, lanes])
            er[slot, :, lanes] = partial(level, row, lanes, scores, gw)
            gr[slot, :, lanes] = gw
            return carry

        lax.fori_loop(0, steps, step, 0, unroll=True)

    def shard_pass(group, place, level):
        low, high, row = group
        keys = slice(low * shard, high * shard)

        def step(j, carry):
            lanes = slice(0, width)
            scores = dot_nn(kv[0, keys], wk[place, 0, :, lanes])
            gw = dot_nn(kv[1, keys], wk[place, 1, :, lanes])
            ep[level, keys, lanes] = partial(level, row, lanes, scores, gw)
            if not lean:
                gp[level, keys, lanes] = gw
            return carry

        lax.fori_loop(0, 1, step, 0, unroll=True)

    stack(sent_local, sent_block, sb)
    pair_q = remote(sb, wk.at[1], pair_send.at[1], pair_recv.at[1], partner)
    pair_q.start()
    pair_kv = remote(
        kv.at[:, own_rows], kv.at[:, own_rows], pair_send.at[0], pair_recv.at[0], partner
    )
    pair_kv.start()
    stack(own_local, own_block, wk.at[0])
    piece(0, core, own_block, core, 2 * core, tail)
    shard_pass(groups[0], 0, core)


    pair_kv.wait_recv()
    pair_q.wait_recv()
    piece(1 - core, 1, blocks_of[1], 0, 1, tail + 1)
    piece(1, 1 - core, other_block, 1 - core, 2 * (1 - core), tail)
    shard_pass(groups[0], 1, 1 - core)

    def forward(low, high):
        rows = slot_rows(low, high)
        return remote(rows, rows, fwd_send.at[0], fwd_recv.at[row_of[low]], partner)

    coming = groups[1 : len(groups) // 2 + 1] + groups[: len(groups) // 2 : -1]
    for i, group in enumerate(coming):
        batch = [group]

        @pl.when(core == 1)
        def _():
            for low, high, _ in batch:
                shards_done(low, high).wait_recv()
                forward(low, high).start()

        @pl.when(core == 0)
        def _():
            forward(*group[:2]).wait_recv()

        for level in range(2):
            shard_pass(group, place_of[level], level)

    for level in range(2):
        rows = slice(0, (tail + 1 + level) * 8)

        def combine(j, carry):
            lanes = lanes_of(j)
            tops = stat[0, level, rows, lanes]
            factors = jnp.exp2((tops - jnp.max(tops, 0, keepdims=True)) * soft)
            inv = 1.0 / jnp.sum(factors * stat[1, level, rows, lanes], 0, keepdims=True)
            inner = jnp.sum(factors * stat[2, level, rows, lanes], 0, keepdims=True) * inv
            fac[level, rows, lanes] = factors * inv
            inn[level, :, lanes] = jnp.broadcast_to(inner, (8, CHUNK))
            return carry

        lax.fori_loop(0, steps, combine, 0, unroll=True)

    def weigh(level, row, lanes, e, gw):
        weights = eighths(e) * fac[level, row * 8 : row * 8 + 8, lanes]
        grads = weights * (eighths(gw) - inn[level, :, lanes])
        return weights.reshape(e.shape).astype(BF16), grads.reshape(e.shape).astype(BF16)

    def scaled(n):
        for level in range(2):
            for k in range(n * per, (n + 1) * per):
                keys = slice(k * shard, (k + 1) * shard)

                def step(j, carry):
                    lanes = lanes_of(j)
                    if lean:
                        gw = dot_nn(kv[1, keys], wk[place_of[level], 1, :, lanes])
                    else:
                        gw = gp[level, keys, lanes]
                    pt[level, keys, lanes], dt[level, keys, lanes] = weigh(
                        level, row_of[k], lanes, ep[level, keys, lanes], gw
                    )
                    return carry

                lax.fori_loop(0, steps, step, 0, unroll=True)

    def totals(weights, grads, items):
        k_sum = v_sum = None
        for i, rows, level in items:
            place = place_of[level]
            k_part = dot_nt(wk[place, 0], grads[i, rows, :])
            v_part = dot_nt(wk[place, 1], weights[i, rows, :])
            k_sum = k_part if k_sum is None else k_sum + k_part
            v_sum = v_part if v_sum is None else v_sum + v_part
        return (k_sum * scale).T, v_sum.T

    per = 256 // shard
    count = chips // per
    sums = {}

    def send_out(n):
        sums[n].wait_recv()
        for k in range((n + 1) * per - 1, n * per - 1, -1):
            if k > 0:
                s2[k] = (tb[core, k] + rb[k]).astype(BF16)
                remote(
                    s2.at[k], r2.at[k], out_send.at[0], out_recv.at[0], {"prompt": source(k)}
                ).start()

    for n in range(count - 1, -1, -1):
        scaled(n)
        rows = slice(n * 256, (n + 1) * 256)
        k_sum, v_sum = totals(pt, dt, [(level, rows, level) for level in range(2)])
        span = pl.ds(n * per, per)
        for which, value in ((0, k_sum), (1, v_sum)):
            value = value.reshape(per, 2, half, 128)
            for c in range(2):
                tb[c, span, which] = value[:, c]
        sums[n] = remote(
            tb.at[1 - core, span], rb.at[span], sum_send.at[n], sum_recv.at[n], partner
        )
        sums[n].start()

        @pl.when(core == 0)
        def _():
            send_out(n)


    @pl.when(core == 1)
    def _():
        for n in range(count - 1, -1, -1):
            send_out(n)

    for slot, level, row in ((0, 0, tail), (1, 1, tail + 1), (2, 1, tail)):

        def reply(j, carry):
            lanes = lanes_of(j)
            pr[slot, :, lanes], dr[slot, :, lanes] = weigh(
                level, row, lanes, er[slot, :, lanes], gr[slot, :, lanes]
            )
            return carry

        lax.fori_loop(0, steps, reply, 0, unroll=True)

    for c, held in ((0, ((0, 0), (1, 1))), (1, ((2, 1),))):
        rt[c, 0], rt[c, 1] = totals(pr, dr, [(slot, slice(None), level) for slot, level in held])
    pair_r = remote(rt.at[1 - core], rr, pair_send.at[2], pair_recv.at[2], partner)
    pair_r.start()

    kt[...] = kv[0].T
    straight = first // 2 == 0

    def grads_step(j, carry):
        lanes = lanes_of(j)
        parts = []
        for level, slots in enumerate(((0,), (1, 2))):
            gq = dot_nn(kt[:, :prefix_len], dt[level, :, lanes])
            for part, slot in enumerate(slots):
                start = prefix_len + part * own_keys
                gq += dot_nn(kt[:, start : start + own_keys], dr[slot, :, lanes])
            parts.append(gq * scale)
        low = jnp.where(straight, parts[0], parts[1])
        high = jnp.where(straight, parts[1], parts[0])
        for s, value in enumerate((low, high)):
            value = value.T
            for i in range(CHUNK // RBLK):
                spot = pl.multiple_of((j * (CHUNK // RBLK) + i) * 128, 128)
                dq[0, s * RBLK : (s + 1) * RBLK, pl.ds(spot, 128)] = value[
                    i * RBLK : (i + 1) * RBLK
                ]
        return carry

    lax.fori_loop(0, steps, grads_step, 0, unroll=True)

    pair_r.wait_recv()
    rk_out[0] = rt[core, 0] + rr[0]
    rv_out[0] = rt[core, 1] + rr[1]

    for sender, slots in ((0, near), (1, far)):

        @pl.when(core == sender)
        def _():
            shards_done(0, len(slots)).wait_send()

    @pl.when(core == 1)
    def _():
        forward(1, chips).wait_send()

    for copy in list(sums.values()) + [pair_kv, pair_q, pair_r]:
        copy.wait_send()

    total = tb[core, 0] + rb[0]
    spread = remote(s2.at[1:chips], r2.at[1:chips], out_send.at[0], out_recv.at[0], partner)
    spread.wait_recv()
    for k in range(1, chips):
        total = total + r2[k].astype(F32)
    pk_out[...] = total[0]
    pv_out[...] = total[1]
    spread.wait_send()


def finish(*refs):
    *refs, sem = refs
    n = len(refs) // 2
    copies = []
    for i in range(n):
        copies.append(pltpu.make_async_copy(refs[i], refs[n + i], sem.at[i]))
    for copy in copies:
        copy.start()
    for copy in copies:
        copy.wait()


def solution(mesh):
    chips = mesh.shape["prompt"]

    def local(
        queries, grad_out, keys_resp, values_resp, keys_prefix, values_prefix, lengths, block_plan
    ):
        slots, width = queries.shape[1:]
        shard, head = keys_prefix.shape
        heads = width // head
        half = shard // 2
        blocks = slots // RBLK
        own_keys = keys_resp.shape[1]
        prefix = chips * shard
        keys = prefix + 2 * own_keys
        lean = prefix > 1024
        count = chips // (256 // shard)
        vm = pltpu.VMEM
        dma = pltpu.SemaphoreType.DMA
        any_spec = pl.BlockSpec(memory_space=pl.ANY)
        vmem = pl.BlockSpec(memory_space=pltpu.VMEM)
        shapes = (
            (1, slots, width),
            (half, head),
            (half, head),
            (1, own_keys, head),
            (1, own_keys, head),
        )
        parts = pl.pallas_call(
            functools.partial(kernel, chips, heads, lean),
            out_shape=tuple(vm(shape, F32) for shape in shapes),
            in_specs=[any_spec] * 8,
            out_specs=(vmem,) * 5,
            scratch_shapes=[
                pltpu.SMEM(lengths.shape, jnp.int32),
                pltpu.SMEM(block_plan.shape, jnp.int32),
                vm((2, blocks, RBLK, width), BF16),
                vm((2, head, width), BF16),
                vm((2, 2, head, width), BF16),
                vm((2, keys, head), BF16),
                vm((head, keys), BF16),
                vm((2, prefix, width), F32),
                vm((2, 8 if lean else prefix, width), F32),
                vm((2, prefix, width), BF16),
                vm((2, prefix, width), BF16),
                vm((3, own_keys, width), BF16),
                vm((3, own_keys, width), BF16),
                vm((3, own_keys, width), F32),
                vm((3, own_keys, width), F32),
                vm((3, 2, (chips // 2 + 3) * 8, width), F32),
                vm((2, (chips // 2 + 3) * 8, width), F32),
                vm((2, 8, width), F32),
                vm((2, chips, 2, half, head), F32),
                vm((chips, 2, half, head), F32),
                vm((chips, 2, half, head), BF16),
                vm((chips, 2, half, head), BF16),
                vm((2, 2, own_keys, head), F32),
                vm((2, own_keys, head), F32),
                dma((5,)),
                dma((3,)),
                dma((3,)),
                dma((1,)),
                dma((chips // 2 + 1,)),
                dma((1,)),
                dma((chips // 2 + 1,)),
                dma((count,)),
                dma((count,)),
                dma((1,)),
                dma((1,)),
            ],
            compiler_params=pltpu.CompilerParams(
                collective_id=0, has_side_effects=True, vmem_limit_bytes=60 * 1024 * 1024
            ),
        )(
            lengths,
            block_plan,
            queries.reshape(blocks, RBLK, width),
            grad_out.reshape(blocks, RBLK, width),
            keys_resp,
            values_resp,
            keys_prefix,
            values_prefix,
        )
        parts = [pltpu.with_memory_space_constraint(part, pltpu.VMEM) for part in parts]
        return pl.pallas_call(
            finish,
            out_shape=tuple(jax.ShapeDtypeStruct(shape, F32) for shape in shapes),
            in_specs=[vmem] * 5,
            out_specs=(any_spec,) * 5,
            scratch_shapes=[dma((5,))],
        )(*parts)

    placed = (
        P(("groups", "prompt"), "resp", None),
        P(("groups", "prompt"), "resp", None),
        P(("groups", "prompt"), "resp", None),
        P(("groups", "prompt"), "resp", None),
        P(("groups", "prompt"), None),
        P(("groups", "prompt"), None),
        P(("groups", "prompt")),
        P(("groups", "prompt"), "resp"),
    )
    return jax.shard_map(
        local,
        mesh=mesh,
        in_specs=placed,
        out_specs=(
            P(("groups", "prompt"), "resp", None),
            P(("groups", "prompt", "resp"), None),
            P(("groups", "prompt", "resp"), None),
            P(("groups", "prompt"), "resp", None),
            P(("groups", "prompt"), "resp", None),
        ),
        check_vma=False,
    )
```
